256 devices in a mesh: section: 2 (over x_hi), lat: 4 (over x_lo, core), lon: 32 (over y, z).
Axes of the slice: x: 4 (x_hi: 2, x_lo: 2; x = x_hi * 2 + x_lo), y: 4, z: 8, core: 2. Of those that a mesh axis runs over, the one named last changes fastest.
Arguments:
- window_input: bfloat16 [2, 16, 2176, 256], P(None, 'lat', 'lon'), may hold values from -8 to 8
- output_cotangent: bfloat16 [2, 16, 2176, 256], P(None, 'lat', 'lon'), may hold values from -6 to 6
- ocean_mask: int32 [16, 2176], P('lat', 'lon'), may hold values 0 or 1
- dw_kernel: bfloat16 [2, 49, 256], P('section'), may hold values from -1.5 to 1.5
- channel_params: bfloat16 [2, 5, 256], P('section'), may hold values from -1.5 to 1.5
- up_weight: bfloat16 [2, 256, 1024], P('section'), may hold values from -0.375 to 0.375
- up_bias: bfloat16 [2, 1024], P('section'), may hold values from -3 to 3
- down_weight: bfloat16 [2, 1024, 256], P('section'), may hold values from -0.1875 to 0.1875
Outputs:
- boundary: bfloat16 [2, 2, 16, 2176, 256], P('section', None, 'lat', 'lon')
- grad_kernel: float32 [2, 49, 256], P('section')
- grad_channels: float32 [2, 5, 256], P('section')
- grad_up: float32 [2, 256, 1024], P('section')
- grad_up_bias: float32 [2, 1024], P('section')
- grad_down: float32 [2, 1024, 256], P('section')
The draws below stay inside these ranges and needn't reach their ends.
All inputs are finite; a program needn't handle non-finite values. No bound on the sum of `ocean_mask` on one device may be relied on, other than what follows from the above.
Results may differ from the reference program's by a relative error of at most 0.012.
Values may be sent and summed in bfloat16 or wider, within the bound.
A program may use at most 128 MiB of HBM per device.

```python
import math
import jax
import jax.numpy as jnp
from jax import lax

C = 256
HID = 1024
KERNEL = 7
ROWS_DEV = 4
COLS_DEV = 68
BATCH = 2
LAT_CELLS = 16
LON_CELLS = 2176
N_SECTION = 2


def rough_values(key, shape):
    return jnp.clip(jax.random.normal(key, shape, jnp.float32), -3.0, 3.0)


def log_spread(key, shape, lowest, highest):
    return jnp.exp(jax.random.uniform(key, shape, jnp.float32, math.log(lowest), math.log(highest)))


def draw_window_input(key, part):
    subkeys = jax.random.split(jax.random.fold_in(key, 11), 3)
    base = rough_values(subkeys[0], (BATCH, LAT_CELLS, LON_CELLS, C))
    cell_scale = log_spread(subkeys[1], (BATCH, LAT_CELLS, LON_CELLS, 1), 0.3, 3.0)
    chan_scale = log_spread(subkeys[2], (1, 1, 1, C), 0.3, 3.0)
    return jnp.clip(base * cell_scale * chan_scale, -8.0, 8.0).astype(jnp.bfloat16)


def draw_dw_kernel(key, part):
    subkeys = jax.random.split(jax.random.fold_in(key, 23), 2)
    base = rough_values(subkeys[0], (N_SECTION, KERNEL * KERNEL, C))
    chan_scale = log_spread(subkeys[1], (N_SECTION, 1, C), 0.05, 0.5)
    return (base * chan_scale).astype(jnp.bfloat16)


def draw_channel_params(key, part):
    subkeys = jax.random.split(jax.random.fold_in(key, 37), 5)
    shape = (N_SECTION, 1, C)
    conv_bias = 0.5 * rough_values(subkeys[0], shape)
    norm_gain = jax.random.uniform(subkeys[1], shape, jnp.float32, 0.6, 1.4)
    norm_shift = 0.3 * rough_values(subkeys[2], shape)
    out_bias = 0.3 * rough_values(subkeys[3], shape)
    layer_scale = log_spread(subkeys[4], shape, 0.2, 1.0)
    return jnp.concatenate([conv_bias, norm_gain, norm_shift, out_bias, layer_scale], axis=1).astype(jnp.bfloat16)


def touch_ends(values, stream_key, low, largest):
    extent = values.shape
    spot = [jax.random.randint(jax.random.fold_in(stream_key, axis), (), 0, extent[axis]) for axis in range(len(extent))]
    values = values.at[tuple(spot)].set(low)
    longest = extent.index(max(extent))
    spot[longest] = (spot[longest] + 1) % extent[longest]
    return values.at[tuple(spot)].set(largest)


def levels(key, shape, cuts, smallest, top_value):
    gain, own = 1.0, jax.random.fold_in(key, 6)
    for position, blocks in cuts:
        heights = jnp.exp(jax.random.uniform(jax.random.fold_in(own, position), (blocks,), jnp.float32, smallest / len(cuts), top_value / len(cuts)))
        gain = gain * jnp.repeat(heights, shape[position] // blocks).reshape([-1 if axis == position else 1 for axis in range(len(shape))])
    return gain


def bell_draw(own_key, dims, scale, most, cuts=(), kind=jnp.bfloat16):
    values = scale * jax.random.normal(own_key, dims, jnp.float32)
    if cuts:
        values = values * levels(own_key, dims, cuts, -0.22, 0.18)
    return jnp.clip(values, -most, most).astype(kind)


def setup_inputs(seed: int = 0) -> dict:
    splits = jax.random.split(jax.random.key(seed), 9)
    return {
        "window_input": draw_window_input(jax.random.fold_in(splits[8], 71), 0),
        "output_cotangent": bell_draw(splits[1], (BATCH, LAT_CELLS, LON_CELLS, C), 1.0, 6.0, ((1, 4), (2, 32))),
        "ocean_mask": touch_ends((jax.random.randint(splits[2], (LAT_CELLS, LON_CELLS), 0, 4) < 3).astype(jnp.int32), jax.random.fold_in(splits[2], 1), 0, 1),
        "dw_kernel": draw_dw_kernel(jax.random.fold_in(splits[8], 71), 0),
        "channel_params": draw_channel_params(jax.random.fold_in(splits[8], 71), 0),
        "up_weight": bell_draw(splits[5], (N_SECTION, C, HID), C ** -0.5, 0.375, ((0, 2),)),
        "up_bias": bell_draw(splits[6], (N_SECTION, HID), 0.5, 3.0, ((0, 2),)),
        "down_weight": bell_draw(splits[7], (N_SECTION, HID, C), HID ** -0.5, 0.1875, ((0, 2),)),
    }


norm_eps = 1e-06
gelu_scale = 0.7978845608028654
gelu_cubic = 0.044715
rows_contract = (((0,), (0,)), ((), ()))
cols_contract = (((1,), (1,)), ((), ()))

def gelu_value(values):
    inner = gelu_scale * (values + gelu_cubic * values * values * values)
    return 0.5 * values * (1.0 + jnp.tanh(inner))

def gelu_slope(values):
    tangent = jnp.tanh(gelu_scale * (values + gelu_cubic * values * values * values))
    return 0.5 * (1.0 + tangent) + 0.5 * values * (1.0 - tangent * tangent) * gelu_scale * (1.0 + 3.0 * gelu_cubic * values * values)

def depthwise(padded, kernel, row_count, col_count):
    summed = jnp.zeros((padded.shape[0], row_count, col_count, padded.shape[3]), jnp.float32)
    for offset in range(KERNEL * KERNEL):
        row_off, col_off = divmod(offset, KERNEL)
        window = padded[:, row_off:row_off + row_count, col_off:col_off + col_count, :]
        summed = summed + window.astype(jnp.float32) * kernel[offset].astype(jnp.float32)
    return summed

def kernel_grads(padded, grad_conv, row_count, col_count):
    channels = grad_conv.shape[-1]
    grad_wide = grad_conv.astype(jnp.float32)
    tap_sums = []
    for offset in range(KERNEL * KERNEL):
        row_off, col_off = divmod(offset, KERNEL)
        window = padded[:, row_off:row_off + row_count, col_off:col_off + col_count, :].astype(jnp.float32)
        tap_sums.append(lax.optimization_barrier(jnp.sum((grad_wide * window).reshape(-1, channels), axis=0)))
    return (jnp.stack(tap_sums), lax.optimization_barrier(jnp.sum(grad_wide.reshape(-1, channels), axis=0)))

def cell_forward(conv_out, inputs, sea_mask, params, w_up, b_up, w_down):
    average = lax.optimization_barrier(jnp.mean(conv_out, axis=-1, keepdims=True))
    centered = conv_out - average
    inverse = lax.rsqrt(lax.optimization_barrier(jnp.mean(centered * centered, axis=-1, keepdims=True)) + norm_eps)
    normed = centered * inverse
    scaled = (normed * params[1].astype(jnp.float32) + params[2].astype(jnp.float32)).astype(jnp.bfloat16)
    channels = scaled.shape[-1]
    flat_rows = scaled.reshape(-1, channels)
    hidden = jnp.dot(flat_rows, w_up, preferred_element_type=jnp.float32) + b_up.astype(jnp.float32)
    active = gelu_value(hidden).astype(jnp.bfloat16)
    branch = jnp.dot(active, w_down, preferred_element_type=jnp.float32) + params[3].astype(jnp.float32)
    branch = branch.reshape(conv_out.shape)
    output = (sea_mask * (inputs.astype(jnp.float32) + params[4].astype(jnp.float32) * branch)).astype(jnp.bfloat16)
    return (output, (normed, inverse, flat_rows, hidden, active, branch))

def cell_backward(saved, sea_mask, cotangent, params, w_up, w_down):
    normed, inverse, flat_rows, hidden, active, branch = saved
    channels = normed.shape[-1]
    upstream = sea_mask * cotangent.astype(jnp.float32)
    grad_scale = lax.optimization_barrier(jnp.sum((upstream * branch).reshape(-1, channels), axis=0))
    grad_branch = (params[4].astype(jnp.float32) * upstream).astype(jnp.bfloat16).reshape(-1, channels)
    grad_down = lax.dot_general(active, grad_branch, rows_contract, preferred_element_type=jnp.float32)
    grad_out_bias = lax.optimization_barrier(jnp.sum(grad_branch.astype(jnp.float32), axis=0))
    grad_active = lax.dot_general(grad_branch, w_down, cols_contract, preferred_element_type=jnp.float32)
    grad_hidden = (grad_active * gelu_slope(hidden)).astype(jnp.bfloat16)
    grad_up = lax.dot_general(flat_rows, grad_hidden, rows_contract, preferred_element_type=jnp.float32)
    grad_up_bias = lax.optimization_barrier(jnp.sum(grad_hidden.astype(jnp.float32), axis=0))
    grad_scaled = lax.dot_general(grad_hidden, w_up, cols_contract, preferred_element_type=jnp.float32)
    grad_scaled = grad_scaled.reshape(normed.shape)
    grad_gain = lax.optimization_barrier(jnp.sum((grad_scaled * normed).reshape(-1, channels), axis=0))
    grad_shift = lax.optimization_barrier(jnp.sum(grad_scaled.reshape(-1, channels), axis=0))
    grad_normed = grad_scaled * params[1].astype(jnp.float32)
    first_mean = lax.optimization_barrier(jnp.mean(grad_normed, axis=-1, keepdims=True))
    second_mean = lax.optimization_barrier(jnp.mean(grad_normed * normed, axis=-1, keepdims=True))
    grad_conv = (inverse * (grad_normed - first_mean - normed * second_mean)).astype(jnp.bfloat16)
    small = (grad_gain, grad_shift, grad_out_bias, grad_scale)
    return (grad_conv, upstream, small, grad_up, grad_up_bias, grad_down)

def pad_field(field):
    reach = KERNEL // 2
    wrapped = jnp.concatenate([field[:, :, field.shape[2] - reach:], field, field[:, :, :reach]], axis=2)
    return jnp.pad(wrapped, ((0, 0), (reach, reach), (0, 0), (0, 0)))

def by_rows(array):
    return jnp.moveaxis(array, 1, 0)

def forward_block(field, sea_rows, weights):
    kernel, params, w_up, b_up, w_down = weights
    padded = pad_field(field)
    conv_out = depthwise(padded, kernel, field.shape[1], field.shape[2]) + params[0].astype(jnp.float32)

    def one_row(pieces):
        conv_row, input_row, mask_row = pieces
        output, unused = cell_forward(conv_row, input_row, mask_row[None, :, None], params, w_up, b_up, w_down)
        return output
    rows_out = lax.map(one_row, (by_rows(conv_out), by_rows(field), sea_rows))
    return jnp.moveaxis(rows_out, 0, 1)

def backward_block(field, sea_rows, weights, cotangent):
    kernel, params, w_up, b_up, w_down = weights
    row_count, col_count = (field.shape[1], field.shape[2])
    channels = field.shape[3]
    hidden_units = w_up.shape[1]
    padded = pad_field(field)
    conv_out = depthwise(padded, kernel, row_count, col_count) + params[0].astype(jnp.float32)
    start = (tuple((jnp.zeros((channels,), jnp.float32) for member in range(4))), jnp.zeros((channels, hidden_units), jnp.float32), jnp.zeros((hidden_units,), jnp.float32), jnp.zeros((hidden_units, channels), jnp.float32))

    def one_row(carry, pieces):
        conv_row, input_row, mask_row, cot_row = pieces
        mask_wide = mask_row[None, :, None]
        output, saved = cell_forward(conv_row, input_row, mask_wide, params, w_up, b_up, w_down)
        grad_conv, upstream, small, grad_up, grad_bias, grad_down = cell_backward(saved, mask_wide, cot_row, params, w_up, w_down)
        carry = jax.tree.map(jnp.add, carry, (small, grad_up, grad_bias, grad_down))
        return (carry, (grad_conv, upstream))
    totals, outputs = lax.scan(one_row, start, (by_rows(conv_out), by_rows(field), sea_rows, by_rows(cotangent)))
    grad_conv = jnp.moveaxis(outputs[0], 0, 1)
    upstream = jnp.moveaxis(outputs[1], 0, 1)
    tap_sums, bias_sum = kernel_grads(padded, grad_conv, row_count, col_count)
    spread = depthwise(pad_field(grad_conv), kernel[::-1], row_count, col_count)
    grad_input = (upstream + spread).astype(jnp.bfloat16)
    small, grad_up, grad_bias, grad_down = totals
    return (grad_input, (tap_sums, jnp.stack((bias_sum,) + tuple(small)), grad_up, grad_bias, grad_down))

def reference(window_input, output_cotangent, ocean_mask, dw_kernel, channel_params, up_weight, up_bias, down_weight):
    sea_rows = ocean_mask.astype(jnp.float32)
    blocks = [(dw_kernel[block_index], channel_params[block_index], up_weight[block_index], up_bias[block_index], down_weight[block_index]) for block_index in range(2)]
    middle = forward_block(window_input, sea_rows, blocks[0])
    final = forward_block(middle, sea_rows, blocks[1])
    grad_middle, grads_second = backward_block(middle, sea_rows, blocks[1], output_cotangent)
    grad_start, grads_first = backward_block(window_input, sea_rows, blocks[0], grad_middle)
    factor = 1.0 / math.sqrt(BATCH * ROWS_DEV * COLS_DEV)
    stacked = jax.tree.map(lambda before, behind: jnp.stack([before, behind]) * factor, grads_first, grads_second)
    boundary = jnp.stack([grad_start, final])
    return (boundary, stacked[0], stacked[1], stacked[2], stacked[3], stacked[4])
```

```python
import math

import jax
import jax.numpy as jnp
from jax import lax
from jax.experimental import pallas as pl
from jax.experimental.pallas import tpu as pltpu
from jax.sharding import PartitionSpec as P

KERNEL = 7
ROWS_DEV = 4
COLS_DEV = 68
BATCH = 2


norm_eps = 1e-06
gelu_scale = 0.7978845608028654
gelu_cubic = 0.044715
rows_contract = (((0,), (0,)), ((), ()))
cols_contract = (((1,), (1,)), ((), ()))


def padded_2(block, sides, width, periodic):
    for axis, dim in sides:
        count = lax.axis_size(axis)
        forward = [(i, i + 1) for i in range(count - 1)]
        if periodic:
            forward.append((count - 1, 0))
        backward = [(target, source) for source, target in forward]
        low = lax.ppermute(
            lax.slice_in_dim(block, block.shape[dim] - width, None, axis=dim), axis, forward
        )
        high = lax.ppermute(lax.slice_in_dim(block, 0, width, axis=dim), axis, backward)
        block = jnp.concatenate([low, block, high], axis=dim)
    return block


def from_behind(value, axis, by):
    count = lax.axis_size(axis)
    pairs = [(i, i + by) for i in range(count) if 0 <= i + by < count]
    return lax.ppermute(value, axis, pairs)


def gelu_value(values):
    inner = gelu_scale * (values + gelu_cubic * values * values * values)
    return 0.5 * values * (1.0 + jnp.tanh(inner))


def gelu_slope(values):
    tangent = jnp.tanh(gelu_scale * (values + gelu_cubic * values * values * values))
    return 0.5 * (1.0 + tangent) + 0.5 * values * (1.0 - tangent * tangent) * gelu_scale * (
        1.0 + 3.0 * gelu_cubic * values * values
    )


def depthwise(padded, kernel, row_count, col_count):
    summed = jnp.zeros((padded.shape[0], row_count, col_count, padded.shape[3]), jnp.float32)
    for offset in range(KERNEL * KERNEL):
        row_off, col_off = divmod(offset, KERNEL)
        window = padded[:, row_off : row_off + row_count, col_off : col_off + col_count, :]
        summed = summed + window.astype(jnp.float32) * kernel[offset].astype(jnp.float32)
    return summed


def kernel_grads(padded, grad_conv, row_count, col_count):
    channels = grad_conv.shape[-1]
    grad_wide = grad_conv.astype(jnp.float32)
    tap_sums = []
    for offset in range(KERNEL * KERNEL):
        row_off, col_off = divmod(offset, KERNEL)
        window = padded[:, row_off : row_off + row_count, col_off : col_off + col_count, :].astype(
            jnp.float32
        )
        tap_sums.append(jnp.sum((grad_wide * window).reshape(-1, channels), axis=0))
    return (jnp.stack(tap_sums), jnp.sum(grad_wide.reshape(-1, channels), axis=0))


def cell_forward(conv_out, inputs, sea_mask, params, w_up, b_up, w_down):
    average = jnp.mean(conv_out, axis=-1, keepdims=True)
    centered = conv_out - average
    inverse = lax.rsqrt(jnp.mean(centered * centered, axis=-1, keepdims=True) + norm_eps)
    normed = centered * inverse
    scaled = (normed * params[1].astype(jnp.float32) + params[2].astype(jnp.float32)).astype(
        jnp.bfloat16
    )
    channels = scaled.shape[-1]
    flat_rows = scaled.reshape(-1, channels)
    hidden = jnp.dot(flat_rows, w_up, preferred_element_type=jnp.float32) + b_up.astype(jnp.float32)
    active = gelu_value(hidden).astype(jnp.bfloat16)
    branch = jnp.dot(active, w_down, preferred_element_type=jnp.float32) + params[3].astype(
        jnp.float32
    )
    branch = branch.reshape(conv_out.shape)
    output = (
        sea_mask * (inputs.astype(jnp.float32) + params[4].astype(jnp.float32) * branch)
    ).astype(jnp.bfloat16)
    return (output, (normed, inverse, flat_rows, hidden, active, branch))


def cell_backward(saved, sea_mask, cotangent, params, w_up, w_down):
    normed, inverse, flat_rows, hidden, active, branch = saved
    channels = normed.shape[-1]
    upstream = sea_mask * cotangent.astype(jnp.float32)
    grad_scale = jnp.sum((upstream * branch).reshape(-1, channels), axis=0)
    grad_branch = (
        (params[4].astype(jnp.float32) * upstream).astype(jnp.bfloat16).reshape(-1, channels)
    )
    grad_down = lax.dot_general(
        active, grad_branch, rows_contract, preferred_element_type=jnp.float32
    )
    grad_out_bias = jnp.sum(grad_branch.astype(jnp.float32), axis=0)
    grad_active = lax.dot_general(
        grad_branch, w_down, cols_contract, preferred_element_type=jnp.float32
    )
    grad_hidden = (grad_active * gelu_slope(hidden)).astype(jnp.bfloat16)
    grad_up = lax.dot_general(
        flat_rows, grad_hidden, rows_contract, preferred_element_type=jnp.float32
    )
    grad_up_bias = jnp.sum(grad_hidden.astype(jnp.float32), axis=0)
    grad_scaled = lax.dot_general(
        grad_hidden, w_up, cols_contract, preferred_element_type=jnp.float32
    )
    grad_scaled = grad_scaled.reshape(normed.shape)
    grad_gain = jnp.sum((grad_scaled * normed).reshape(-1, channels), axis=0)
    grad_shift = jnp.sum(grad_scaled.reshape(-1, channels), axis=0)
    grad_normed = grad_scaled * params[1].astype(jnp.float32)
    first_mean = jnp.mean(grad_normed, axis=-1, keepdims=True)
    second_mean = jnp.mean(grad_normed * normed, axis=-1, keepdims=True)
    grad_conv = (inverse * (grad_normed - first_mean - normed * second_mean)).astype(jnp.bfloat16)
    small = (grad_gain, grad_shift, grad_out_bias, grad_scale)
    return (grad_conv, upstream, small, grad_up, grad_up_bias, grad_down)


def halo_field(field):
    reach = KERNEL // 2
    beside_all = padded_2(field, (("lon", 2),), reach, True)
    return padded_2(beside_all, (("lat", 1),), reach, False)


def run_forward(field, sea_mask, weights):
    kernel, params, w_up, b_up, w_down = weights
    padded = halo_field(field)
    conv_out = depthwise(padded, kernel, field.shape[1], field.shape[2]) + params[0].astype(
        jnp.float32
    )
    output, saved = cell_forward(conv_out, field, sea_mask, params, w_up, b_up, w_down)
    return (output, (padded, saved))


def run_backward(stored, sea_mask, weights, cotangent):
    kernel, params, w_up, b_up, w_down = weights
    padded, saved = stored
    row_count, col_count = (cotangent.shape[1], cotangent.shape[2])
    grad_conv, upstream, small, grad_up, grad_bias, grad_down = cell_backward(
        saved, sea_mask, cotangent, params, w_up, w_down
    )
    tap_sums, bias_sum = kernel_grads(padded, grad_conv, row_count, col_count)
    spread = depthwise(halo_field(grad_conv), kernel[::-1], row_count, col_count)
    grad_input = (upstream + spread).astype(jnp.bfloat16)
    return (grad_input, (tap_sums, jnp.stack((bias_sum,) + small), grad_up, grad_bias, grad_down))


MESH = pl.DeviceIdType.MESH
N_Y = 4
N_Z = 8


def sum_kernel(part, out, r_core, q_half, r_y, t_all, r_z, u_all, r_x, send, recv):
    lat = lax.axis_index("lat")
    lon = lax.axis_index("lon")
    x, core = lat // 2, lat % 2
    y, z = lon // N_Z, lon % N_Z

    sibling = {"lat": x * 2 + (1 - core)}
    across = {"lat": (1 - x) * 2 + core}

    def y_peer(d):
        return {"lon": (y + d) % N_Y * N_Z + z}

    def z_peer(d):
        return {"lon": y * N_Z + (z + d) % N_Z}

    peers = [sibling, across] + [y_peer(d) for d in range(1, N_Y)] + [z_peer(d) for d in range(1, N_Z)]
    barrier = pltpu.get_barrier_semaphore()
    for peer in peers:
        pl.semaphore_signal(barrier, inc=1, device_id=peer, device_id_type=MESH)
    pl.semaphore_wait(barrier, len(peers))

    def push(source, target, slot, peer):
        copy = pltpu.make_async_remote_copy(
            src_ref=source,
            dst_ref=target,
            send_sem=send.at[slot],
            recv_sem=recv.at[slot],
            device_id=peer,
            device_id_type=MESH,
        )
        copy.start()
        return copy

    c0 = push(part.at[1 - core], r_core, 0, sibling)
    c0.wait()
    for k in range(N_Y):
        q_half[k] = (part[core, k].astype(jnp.float32) + r_core[k].astype(jnp.float32)).astype(jnp.bfloat16)
    copies = [push(q_half.at[(y + d) % N_Y], r_y.at[d - 1], d, y_peer(d)) for d in range(1, N_Y)]
    for copy in copies:
        copy.wait()

    def y_sum(rows):
        total = q_half[y, rows].astype(jnp.float32)
        for d in range(1, N_Y):
            total = total + r_y[d - 1, rows].astype(jnp.float32)
        return total.astype(jnp.bfloat16)

    tail = y_sum(pl.ds(512, 16))
    for k in range(N_Z):
        t_all[k, 0:64] = y_sum(pl.ds(64 * k, 64))
        t_all[k, 64:80] = tail
    copies = [push(t_all.at[(z + d) % N_Z], r_z.at[d - 1], 3 + d, z_peer(d)) for d in range(1, N_Z)]
    for copy in copies:
        copy.wait()

    def z_sum(low, size):
        total = jnp.zeros((size, 128), jnp.float32)
        me = t_all[z, low : low + size].astype(jnp.float32)
        total = total + me
        for d in range(1, N_Z):
            total = total + r_z[d - 1, low : low + size].astype(jnp.float32)
        return total.astype(jnp.bfloat16)

    tail = z_sum(64, 16)
    for k in range(2):
        u_all[k, 0:32] = z_sum(32 * k, 32)
        u_all[k, 32:48] = tail
    c = push(u_all.at[1 - x], r_x, 11, across)
    c.wait()
    mine = (u_all[x].astype(jnp.float32) + r_x[...].astype(jnp.float32)).astype(jnp.bfloat16)
    own = pl.multiple_of(64 * z + 32 * x, 32)
    out[core, y, pl.ds(own, 32)] = mine[0:32]
    out[core, y, pl.ds(512, 16)] = mine[32:48]
    spot = out.at[core, y, pl.ds(own, 32)]
    c = push(spot, spot, 12, across)
    c.wait()
    spot = out.at[core, y, pl.ds(pl.multiple_of(64 * z, 64), 64)]
    copies = [push(spot, spot, 12 + d, z_peer(d)) for d in range(1, N_Z)]
    for copy in copies:
        copy.wait()
    spot = out.at[core, y]
    copies = [push(spot, spot, 19 + d, y_peer(d)) for d in range(1, N_Y)]
    for copy in copies:
        copy.wait()
    spot = out.at[core]
    c = push(spot, spot, 23, sibling)
    c.wait()


def sum_over_band(taps, chans, up, up_bias, down):
    small = jnp.concatenate([taps, chans, up_bias.reshape(4, 256)], axis=0).reshape(-1, 128)
    small = jnp.pad(small, ((0, 128 - small.shape[0]), (0, 0))).reshape(8, 16, 128)
    packed = jnp.concatenate(
        [
            up.reshape(256, 8, 128).transpose(1, 0, 2),
            down.reshape(8, 128, 2, 128).transpose(0, 2, 1, 3).reshape(8, 256, 128),
            small,
        ],
        axis=1,
    ).astype(jnp.bfloat16).reshape(2, 4, 528, 128)
    summed = pl.pallas_call(
        sum_kernel,
        out_shape=jax.ShapeDtypeStruct((2, 4, 528, 128), jnp.bfloat16),
        in_specs=[pl.BlockSpec(memory_space=pltpu.VMEM)],
        out_specs=pl.BlockSpec(memory_space=pltpu.VMEM),
        scratch_shapes=[
            pltpu.VMEM((4, 528, 128), jnp.bfloat16),
            pltpu.VMEM((4, 528, 128), jnp.bfloat16),
            pltpu.VMEM((3, 528, 128), jnp.bfloat16),
            pltpu.VMEM((8, 80, 128), jnp.bfloat16),
            pltpu.VMEM((7, 80, 128), jnp.bfloat16),
            pltpu.VMEM((2, 48, 128), jnp.bfloat16),
            pltpu.VMEM((48, 128), jnp.bfloat16),
            pltpu.SemaphoreType.DMA((24,)),
            pltpu.SemaphoreType.DMA((24,)),
        ],
        compiler_params=pltpu.CompilerParams(
            collective_id=0, has_side_effects=True, vmem_limit_bytes=40 << 20
        ),
        name="band_sum",
    )(packed)
    wide = summed.astype(jnp.float32).reshape(8, 528, 128)
    up_sum = wide[:, :256].transpose(1, 0, 2).reshape(256, 1024)
    down_sum = wide[:, 256:512].reshape(8, 2, 128, 128).transpose(0, 2, 1, 3).reshape(1024, 256)
    small = wide[:, 512:].reshape(128, 128)[:116].reshape(58, 256)
    return (small[:49], small[49:54], up_sum, small[54:].reshape(1024), down_sum)


def on_device(
    window_input,
    output_cotangent,
    ocean_mask,
    dw_kernel,
    channel_params,
    up_weight,
    up_bias,
    down_weight,
):
    section = lax.axis_index("section")
    first_section = section == 0
    sea_mask = ocean_mask.astype(jnp.float32)[None, :, :, None]
    batch_size = window_input.shape[0]
    local = (dw_kernel[0], channel_params[0], up_weight[0], up_bias[0], down_weight[0])
    micro = 1
    size_micro = batch_size // micro
    zero_field = jnp.zeros((size_micro,) + window_input.shape[1:], jnp.bfloat16)
    received = zero_field
    stored = []
    outputs = []
    for tick in range(micro + 1):
        if tick < micro:
            own_part = window_input
        else:
            own_part = zero_field
        current = jnp.where(first_section, own_part, received)
        result, kept = run_forward(current, sea_mask, local)
        stored.append(kept)
        outputs.append(result)
        if tick < micro:
            received = from_behind(result, "section", 1)
    received = zero_field
    grad_inputs = []
    totals = None
    for tick in range(micro + 1):
        if tick < micro:
            own_part = output_cotangent
        else:
            own_part = zero_field
        current = jnp.where(first_section, received, own_part)
        kept = jax.tree.map(
            lambda before, behind: jnp.where(first_section, before, behind),
            stored[max(tick - 1, 0)],
            stored[min(tick + 1, micro)],
        )
        grad_input, grads = run_backward(kept, sea_mask, local, current)
        counted = jnp.where(
            first_section, 1.0 if tick >= 1 else 0.0, 1.0 if tick < micro else 0.0
        ).astype(jnp.float32)
        weighted = jax.tree.map(lambda member: member * counted, grads)
        if totals is None:
            totals = weighted
        else:
            totals = jax.tree.map(jnp.add, totals, weighted)
        grad_inputs.append(grad_input)
        if tick < micro:
            received = from_behind(grad_input, "section", -1)
    final = jnp.concatenate(outputs[1:], axis=0)
    starts = jnp.concatenate(grad_inputs[1:], axis=0)
    boundary = jnp.where(first_section, starts, final)[None]
    summed = tuple(member[None] for member in sum_over_band(*totals))
    factor = 1.0 / math.sqrt(BATCH * ROWS_DEV * COLS_DEV)
    return (
        boundary,
        summed[0] * factor,
        summed[1] * factor,
        summed[2] * factor,
        summed[3] * factor,
        summed[4] * factor,
    )


def solution(mesh):
    in_specs = (
        P(None, "lat", "lon", None),
        P(None, "lat", "lon", None),
        P("lat", "lon"),
        P("section", None, None),
        P("section", None, None),
        P("section", None, None),
        P("section", None),
        P("section", None, None),
    )
    out_specs = (
        P("section", None, "lat", "lon", None),
        P("section", None, None),
        P("section", None, None),
        P("section", None, None),
        P("section", None),
        P("section", None, None),
    )
    return jax.shard_map(
        on_device, mesh=mesh, in_specs=in_specs, out_specs=out_specs, check_vma=False
    )
```

```python
import functools
import math

import jax
import jax.numpy as jnp
from jax import lax
from jax.experimental import pallas as pl
from jax.experimental.pallas import tpu as pltpu
from jax.sharding import PartitionSpec as P

MESH = pl.DeviceIdType.MESH
F32 = jnp.float32
BF16 = jnp.bfloat16
N_LAT = 4
N_LON = 32
N_Y = 4
N_Z = 8
COLS = 17
ROWS = 16
CELLS = COLS * ROWS
PART = 68
EDGE = 3 * ROWS
C = 256
BIG = 512
SLAB = 544

norm_eps = 1e-06
gelu_scale = 0.7978845608028654
gelu_cubic = 0.044715
factor = 1.0 / math.sqrt(544)
rows_contract = (((0,), (0,)), ((), ()))
cols_contract = (((1,), (1,)), ((), ()))

S_SMALL, S_UP, S_DOWN, S_UPF, S_DOWNF = 0, 1, 2, 3, 4
S_X, S_M, S_C = 5, 8, 11
S_HALO = 14
S_OWN, S_CROSS = 22, 26
S_SUM = 30
L_CORE, L_CORES, L_Y, L_YS, L_Z, L_XA, L_XB = 0, 1, 2, 5, 8, 15, 16
N_SUM = 18
S_GX = S_SUM + 2 * N_SUM
S_GZ, S_GY, S_GC = S_GX + 1, S_GX + 8, S_GX + 11
N_SEM = S_GX + 12
D_UP, D_DOWN, D_SMALL = 0, 1, 2


def step_kernel(
    x_ref, c_ref, m_ref, sw_ref, up_ref, down_ref,
    out_ref, gup_ref, gdown_ref, gsmall_ref,
    w_up, w_down, w_sm, w32,
    xs, cs, a_x, a_c, a_m, t2, s2,
    dense, mask, pad, shifted, edge_out, edge_in,
    u_buf, normed, inv, z_buf, act, slope, branch, e_buf, dm_buf, du_buf, cot,
    slabs, small, r_core, half, r_y, r_z, t_all, u_all, r_x, full,
    o_send, o_recv, o32,
    local, send, recv,
):
    sec = lax.axis_index("section")
    lat = lax.axis_index("lat")
    lon = lax.axis_index("lon")
    x, core = lat // 2, lat % 2
    y, z = lon // N_Z, lon % N_Z

    sibling = {"lat": x * 2 + (1 - core)}
    across = {"lat": (1 - x) * 2 + core}
    partner = {"section": 1 - sec, "lat": (1 - x) * 2 + core}
    right = {"lat": (lat + 1) % N_LAT, "lon": (lon + (lat + 1) // N_LAT) % N_LON}
    left = {"lat": (lat + 3) % N_LAT, "lon": (lon + N_LON - 1 + (lat + 3) // N_LAT) % N_LON}

    def lat_peer(d):
        return {"lat": (lat + d) % N_LAT}

    def cross_peer(d):
        return {"section": 1 - sec, "lat": (lat + d) % N_LAT}

    def y_peer(d):
        return {"lon": (y + d) % N_Y * N_Z + z}

    def z_peer(d):
        return {"lon": y * N_Z + (z + d) % N_Z}

    def remote(source, target, slot, peer):
        return pltpu.make_async_remote_copy(
            src_ref=source,
            dst_ref=target,
            send_sem=send.at[slot],
            recv_sem=recv.at[slot],
            device_id=peer,
            device_id_type=MESH,
        )

    def push(source, target, slot, peer):
        copy = remote(source, target, slot, peer)
        copy.start()
        return copy

    def strips(field_ref, target):
        for h in range(2):
            lanes = slice(128 * h, 128 * (h + 1))
            for r in range(4):
                t2[h, pl.ds(r, PART, stride=4), :] = field_ref[sec, r, :, lanes].astype(F32)
            for b in range(N_LAT):
                target[b, :, lanes] = t2[h, PART * b : PART * (b + 1), :].astype(BF16)

    strips(x_ref, xs)
    strips(c_ref, cs)

    peers = [lat_peer(d) for d in range(1, 4)] + [cross_peer(d) for d in range(4)] + [left, right]
    peers += [y_peer(d) for d in range(1, N_Y)] + [z_peer(d) for d in range(1, N_Z)]
    barrier = pltpu.get_barrier_semaphore()
    for peer in peers:
        pl.semaphore_signal(barrier, inc=1, device_id=peer, device_id_type=MESH)
    pl.semaphore_wait(barrier, len(peers))

    pending = []

    def later(copy):
        pending.append(copy)
        return copy

    x_in = [later(push(xs.at[(lat + d) % 4], a_x.at[lat], S_X + d - 1, lat_peer(d))) for d in range(1, 4)]
    m_in = [later(push(m_ref.at[(lat + d) % 4], a_m.at[lat], S_M + d - 1, lat_peer(d))) for d in range(1, 4)]
    sm_in = later(push(sw_ref, w_sm.at[sec], S_SMALL, partner))
    own_up = pltpu.make_async_copy(up_ref, w_up.at[sec], local.at[D_UP])
    own_down = pltpu.make_async_copy(down_ref, w_down.at[sec], local.at[D_DOWN])
    own_up.start()
    own_down.start()
    up_rows = pl.ds(pl.multiple_of(core * 128, 128), 128)
    down_rows = pl.ds(pl.multiple_of(core * 512, 512), 512)
    up_in = later(push(up_ref.at[up_rows], w_up.at[sec, up_rows], S_UP, partner))
    down_in = later(push(down_ref.at[down_rows], w_down.at[sec, down_rows], S_DOWN, partner))
    c_in = [later(push(cs.at[(lat + d) % 4], a_c.at[lat], S_C + d - 1, lat_peer(d))) for d in range(1, 4)]

    a_x[lat] = xs[lat]
    a_c[lat] = cs[lat]
    a_m[lat] = m_ref[lat]
    w_sm[sec] = sw_ref[...]
    pad[:, 0:8, :] = jnp.zeros((COLS + 6, 8, C), F32)
    pad[:, 24:32, :] = jnp.zeros((COLS + 6, 8, C), F32)
    small[...] = jnp.zeros_like(small)

    def gather(parts, target, lanes):
        for h in range(lanes // 128):
            cut = slice(128 * h, 128 * (h + 1))
            for a in range(N_LAT):
                t2[h, PART * a : PART * (a + 1), :] = parts[a, :, cut].astype(F32)
            for a in range(N_LAT):
                for r in range(4):
                    s2[h, pl.ds(4 * a + r, COLS, stride=ROWS), :] = t2[h, pl.ds(PART * a + r, COLS, stride=4), :]
            target[:, cut] = s2[h]

    def halo_start(field, number):
        edge_out[number, 0] = field[CELLS - EDGE : CELLS, :].astype(BF16)
        edge_out[number, 1] = field[0:EDGE, :].astype(BF16)
        base = S_HALO + 2 * number
        return [
            push(edge_out.at[number, 0], edge_in.at[number, 0], base, right),
            push(edge_out.at[number, 1], edge_in.at[number, 1], base + 1, left),
        ]

    def halo_end(field, copies, number, slot):
        for j in range(COLS):
            pad[3 + j, 8:24, :] = field[ROWS * j : ROWS * (j + 1), :]
        for copy in copies:
            copy.wait()
        for j in range(3):
            rows = slice(ROWS * j, ROWS * (j + 1))
            pad[j, 8:24, :] = edge_in[number, 0, rows, :].astype(F32)
            pad[COLS + 3 + j, 8:24, :] = edge_in[number, 1, rows, :].astype(F32)

        def shift(col, carry):
            for p in range(7):
                shifted[slot, p, col] = pad[col, 5 + p : 21 + p, :]
            return carry

        lax.fori_loop(0, COLS + 6, shift, 0)

    def stencil(slot, k, reverse, target):
        for h in range(2):
            lanes = slice(128 * h, 128 * (h + 1))

            def tap_row(p, acc):
                taps = w32[k, pl.ds(pl.multiple_of(8 * ((6 - p) if reverse else p), 8), 8), lanes]
                for q in range(7):
                    row = 6 - q if reverse else q
                    window = shifted[slot, p, q : q + COLS, :, lanes]
                    acc = acc + window * taps[row : row + 1, :][None]
                return acc

            acc = lax.fori_loop(0, 7, tap_row, jnp.zeros((COLS, ROWS, 128), F32))
            target[:, lanes] = acc.reshape(CELLS, 128)

    def tap_grads(k):
        for h in range(2):
            lanes = slice(128 * h, 128 * (h + 1))

            def tap_row(p, carry):
                grad = du_buf[:, lanes].reshape(COLS, ROWS, 128)
                for q in range(7):
                    window = shifted[k, p, q : q + COLS, :, lanes]
                    total = jnp.sum((grad * window).reshape(CELLS, 128), axis=0, keepdims=True)
                    small[p, 8 * h + q : 8 * h + q + 1, :] = total
                return carry

            lax.fori_loop(0, 7, tap_row, 0)

    def wide_mask():
        return jnp.concatenate([mask[...], mask[...]], axis=1)

    def normalise(k):
        u = u_buf[...] + w32[k, 56:57, :]
        centered = u - jnp.mean(u, axis=-1, keepdims=True)
        inverse = lax.rsqrt(jnp.mean(centered * centered, axis=-1, keepdims=True) + norm_eps)
        value = centered * inverse
        inv[k] = inverse
        normed[k] = value
        z_buf[k] = (value * w32[k, 57:58, :] + w32[k, 58:59, :]).astype(BF16)

    def mlp_hidden(k):
        def chunk(i, carry):
            cols = pl.ds(pl.multiple_of(256 * i, 256), 256)
            hidden = jnp.dot(z_buf[k], w_up[k, :, cols], preferred_element_type=F32)
            hidden = hidden + w32[k, pl.ds(64 + i, 1), :]
            square = hidden * hidden
            tangent = jnp.tanh(gelu_scale * (hidden + gelu_cubic * square * hidden))
            act[k, :, cols] = (0.5 * hidden * (1.0 + tangent)).astype(BF16)
            slope[k, :, cols] = 0.5 * (1.0 + tangent) + 0.5 * hidden * (1.0 - tangent * tangent) * gelu_scale * (
                1.0 + 3.0 * gelu_cubic * square
            )
            return carry

        lax.fori_loop(0, 4, chunk, 0)

    def mlp_out(k, target):
        value = jnp.dot(act[k], w_down[k], preferred_element_type=F32) + w32[k, 59:60, :]
        branch[k] = value
        result = wide_mask() * (dense[...] + w32[k, 60:61, :] * value)
        target[...] = result.astype(BF16).astype(F32)

    def put_small(row, total):
        small[0, row : row + 1, :] = total[:, 0:128]
        small[1, row : row + 1, :] = total[:, 128:256]

    def mlp_back(k):
        e = wide_mask() * cot[...]
        e_buf[...] = e
        put_small(28, jnp.sum(e * branch[k], axis=0, keepdims=True))
        dm_wide = (w32[k, 60:61, :] * e).astype(BF16)
        dm_buf[...] = dm_wide
        put_small(27, jnp.sum(dm_wide.astype(F32), axis=0, keepdims=True))
        u_buf[...] = jnp.zeros((CELLS, C), F32)

        def chunk(i, carry):
            cols = pl.ds(pl.multiple_of(256 * i, 256), 256)
            dm = dm_buf[...]
            da = lax.dot_general(dm, w_down[k, cols, :], cols_contract, preferred_element_type=F32)
            dh = (da * slope[k, :, cols]).astype(BF16)
            bias = jnp.sum(dh.astype(F32), axis=0, keepdims=True)
            u_buf[...] += lax.dot_general(dh, w_up[k, :, cols], cols_contract, preferred_element_type=F32)
            gup = lax.dot_general(z_buf[k], dh, rows_contract, preferred_element_type=F32).astype(BF16)
            gdown = lax.dot_general(act[k, :, cols], dm, rows_contract, preferred_element_type=F32).astype(BF16)
            for t in range(2):
                slab = 2 * i + t
                cut = slice(128 * t, 128 * (t + 1))
                small[slab, 16:17, :] = bias[:, cut]
                slabs[k, slab, 0:256, :] = gup[:, cut]
                slabs[k, slab, 256:384, :] = gdown[cut, 0:128]
                slabs[k, slab, 384:512, :] = gdown[cut, 128:256]
            return carry

        lax.fori_loop(0, 4, chunk, 0)
        dz = u_buf[...]
        put_small(25, jnp.sum(dz * normed[k], axis=0, keepdims=True))
        put_small(26, jnp.sum(dz, axis=0, keepdims=True))
        dn = dz * w32[k, 57:58, :]
        first = jnp.mean(dn, axis=-1, keepdims=True)
        second = jnp.mean(dn * normed[k], axis=-1, keepdims=True)
        du = (inv[k] * (dn - first - normed[k] * second)).astype(BF16).astype(F32)
        du_buf[...] = du
        put_small(24, jnp.sum(du, axis=0, keepdims=True))

    other = pl.ds(4 * (1 - core), 4)
    mine4 = 4 * core

    def sem(k, number):
        return S_SUM + N_SUM * k + number

    def core_big(k):
        return push(slabs.at[k, other, pl.ds(0, BIG)], r_core.at[k, :, pl.ds(0, BIG)], sem(k, L_CORE), sibling)

    def core_small(k):
        for slab in range(8):
            slabs[k, slab, BIG:SLAB, :] = small[slab].astype(BF16)
        return push(slabs.at[k, other, pl.ds(BIG, 32)], r_core.at[k, :, pl.ds(BIG, 32)], sem(k, L_CORES), sibling)

    def y_phase(k, copy, low, size, number):
        copy.wait()
        rows = slice(low, low + size)

        def add(i, carry):
            total = slabs[k, mine4 + i, rows, :].astype(F32) + r_core[k, i, rows, :].astype(F32)
            half[k, i, rows, :] = total.astype(BF16)
            return carry

        lax.fori_loop(0, 4, add, 0)
        return [
            push(
                half.at[k, (y + d) % N_Y, pl.ds(low, size)],
                r_y.at[k, d - 1, pl.ds(low, size)],
                sem(k, number + d - 1),
                y_peer(d),
            )
            for d in range(1, N_Y)
        ]

    def z_phase(k, copies):
        for copy in copies:
            copy.wait()

        def y_sum(rows):
            total = half[k, y, rows, :].astype(F32)
            for d in range(3):
                total = total + r_y[k, d, rows, :].astype(F32)
            return total.astype(BF16)

        tail = y_sum(slice(BIG, SLAB))
        for i in range(N_Z):
            t_all[k, i, 0:64, :] = y_sum(slice(64 * i, 64 * (i + 1)))
            t_all[k, i, 64:96, :] = tail
        sent = [
            push(t_all.at[k, (z + d) % N_Z], r_z.at[k, z], sem(k, L_Z + d - 1), z_peer(d)) for d in range(1, N_Z)
        ]
        r_z[k, z] = t_all[k, z]
        return sent

    def x_phase(k, copies):
        for copy in copies:
            copy.wait()

        def z_sum(low, size):
            total = r_z[k, 0, low : low + size, :].astype(F32)
            for i in range(1, N_Z):
                total = total + r_z[k, i, low : low + size, :].astype(F32)
            return total.astype(BF16)

        tail = z_sum(64, 32)
        for i in range(2):
            u_all[k, i, 0:32, :] = z_sum(32 * i, 32)
            u_all[k, i, 32:64, :] = tail

        @pl.when(sec == k)
        def _():
            r_x[k, 2 * k + x] = u_all[k, x]
            push(u_all.at[k, 1 - x], r_x.at[k, 2 * k + x], sem(k, L_XA), across)

        @pl.when(sec != k)
        def _():
            for f in range(2):
                owner = (x + f) % 2
                push(
                    u_all.at[k, owner],
                    r_x.at[k, 2 * (1 - k) + x],
                    sem(k, L_XB + f),
                    {"section": 1 - sec, "lat": owner * 2 + core},
                )

    my_slab = 4 * core + y
    own_rows = pl.ds(pl.multiple_of(64 * z + 32 * x, 32), 32)

    def x_end(k):
        @pl.when(sec == k)
        def _():
            remote(u_all.at[k, 1 - x], r_x.at[k, 2 * k + x], sem(k, L_XA), across).wait()
            for f in range(2):
                remote(u_all.at[k, 0], r_x.at[k, 2 * (1 - k) + f], sem(k, L_XB + f), partner).wait_recv()
            total = r_x[k, 0].astype(F32)
            for i in range(1, 4):
                total = total + r_x[k, i].astype(F32)
            total = total.astype(BF16)
            full[my_slab, own_rows, :] = total[0:32]
            full[my_slab, BIG:SLAB, :] = total[32:64]
            spot = full.at[my_slab, own_rows]
            push(spot, spot, S_GX, across)

        @pl.when(sec != k)
        def _():
            for f in range(2):
                remote(u_all.at[k, 0], r_x.at[k, 2 * (1 - k) + f], sem(k, L_XB + f), partner).wait_send()

    def gather_z(k):
        @pl.when(sec == k)
        def _():
            spot = full.at[my_slab, own_rows]
            remote(spot, spot, S_GX, across).wait()
            spot = full.at[my_slab, pl.ds(pl.multiple_of(64 * z, 64), 64)]
            for d in range(1, N_Z):
                push(spot, spot, S_GZ + d - 1, z_peer(d))

    def gather_y(k):
        @pl.when(sec == k)
        def _():
            spot = full.at[my_slab, pl.ds(pl.multiple_of(64 * z, 64), 64)]
            for d in range(1, N_Z):
                remote(spot, spot, S_GZ + d - 1, z_peer(d)).wait()
            for d in range(1, N_Y):
                push(full.at[my_slab], full.at[my_slab], S_GY + d - 1, y_peer(d))

    def gather_core(k):
        @pl.when(sec == k)
        def _():
            for d in range(1, N_Y):
                remote(full.at[my_slab], full.at[my_slab], S_GY + d - 1, y_peer(d)).wait()
            spot = full.at[pl.ds(mine4, 4)]
            push(spot, spot, S_GC, sibling)

    def gather_end(k):
        @pl.when(sec == k)
        def _():
            spot = full.at[pl.ds(mine4, 4)]
            remote(spot, spot, S_GC, sibling).wait()

            def put(i, carry):
                cols = pl.ds(pl.multiple_of(128 * i, 128), 128)
                gup_ref[:, cols] = full[i, 0:256, :].astype(F32) * factor
                gdown_ref[cols, 0:128] = full[i, 256:384, :].astype(F32) * factor
                gdown_ref[cols, 128:256] = full[i, 384:512, :].astype(F32) * factor
                gsmall_ref[i] = full[i, BIG:SLAB, :].astype(F32) * factor
                return carry

            lax.fori_loop(0, 8, put, 0)

    def out_start(k, field):
        for h in range(2):
            cut = slice(128 * h, 128 * (h + 1))
            s2[h] = field[:, cut]
            for a in range(N_LAT):
                for r in range(4):
                    t2[h, pl.ds(PART * a + r, COLS, stride=4), :] = s2[h, pl.ds(4 * a + r, COLS, stride=ROWS), :]
                o_send[k, a, :, cut] = t2[h, PART * a : PART * (a + 1), :].astype(BF16)

        @pl.when(sec == k)
        def _():
            o_recv[k, lat] = o_send[k, lat]
            for d in range(1, 4):
                push(o_send.at[k, (lat + d) % 4], o_recv.at[k, lat], S_OWN + d, lat_peer(d))

        @pl.when(sec != k)
        def _():
            for d in range(4):
                push(o_send.at[k, (lat + d) % 4], o_recv.at[1 - k, lat], S_CROSS + d, cross_peer(d))

    def out_end(k):
        @pl.when(sec == k)
        def _():
            for d in range(1, 4):
                remote(o_send.at[k, 0], o_recv.at[k, (lat + 4 - d) % 4], S_OWN + d, lat_peer(d)).wait()
            for d in range(4):
                remote(o_send.at[k, 0], o_recv.at[1 - k, (lat + 4 - d) % 4], S_CROSS + d, lat_peer(1)).wait_recv()
            for sample in range(2):
                for h in range(2):
                    cut = slice(128 * h, 128 * (h + 1))
                    for b in range(N_LAT):
                        t2[h, PART * b : PART * (b + 1), :] = o_recv[sample, b, :, cut].astype(F32)
                    for b in range(N_LAT):
                        for r in range(4):
                            o32[r, COLS * b : COLS * (b + 1), cut] = t2[h, pl.ds(PART * b + r, COLS, stride=4), :]
                out_ref[sample] = o32[...].astype(BF16)

        @pl.when(sec != k)
        def _():
            for d in range(4):
                remote(o_send.at[k, 0], o_recv.at[1 - k, 0], S_CROSS + d, cross_peer(d)).wait_send()

    for copy in x_in + m_in:
        copy.wait()
    gather(a_x, dense, 256)
    copies = halo_start(dense, 0)
    gather(a_m, mask, 128)
    sm_in.wait()
    for k in range(2):
        w32[k] = w_sm[k].astype(F32)
    halo_end(dense, copies, 0, 0)
    stencil(0, 0, False, u_buf)
    normalise(0)
    up_in.wait()
    their_up = w_up.at[1 - sec, up_rows]
    up_fwd = push(their_up, their_up, S_UPF, sibling)
    own_up.wait()
    up_fwd.wait()
    mlp_hidden(0)
    down_in.wait()
    their_down = w_down.at[1 - sec, down_rows]
    down_fwd = push(their_down, their_down, S_DOWNF, sibling)
    own_down.wait()
    down_fwd.wait()
    mlp_out(0, cot)
    dense[...] = cot[...]
    copies = halo_start(dense, 1)
    halo_end(dense, copies, 1, 1)
    stencil(1, 1, False, u_buf)
    normalise(1)
    mlp_hidden(1)
    mlp_out(1, cot)
    out_start(1, cot)

    for copy in c_in:
        copy.wait()
    gather(a_c, cot, 256)
    mlp_back(1)
    copies = halo_start(du_buf, 2)
    sum1 = core_big(1)
    tap_grads(1)
    sum1s = core_small(1)
    sum1 = y_phase(1, sum1, 0, BIG, L_Y)
    halo_end(du_buf, copies, 2, 2)
    stencil(2, 1, True, u_buf)
    cot[...] = (e_buf[...] + u_buf[...]).astype(BF16).astype(F32)
    sum1 = sum1 + y_phase(1, sum1s, BIG, 32, L_YS)

    mlp_back(0)
    copies = halo_start(du_buf, 3)
    sum0 = core_big(0)
    sum1 = z_phase(1, sum1)
    tap_grads(0)
    sum0s = core_small(0)
    sum0 = y_phase(0, sum0, 0, BIG, L_Y)
    x_phase(1, sum1)
    halo_end(du_buf, copies, 3, 2)
    stencil(2, 0, True, u_buf)
    cot[...] = (e_buf[...] + u_buf[...]).astype(BF16).astype(F32)
    out_start(0, cot)
    sum0 = sum0 + y_phase(0, sum0s, BIG, 32, L_YS)
    x_end(1)
    sum0 = z_phase(0, sum0)
    gather_z(1)
    out_end(1)
    x_phase(0, sum0)
    gather_y(1)
    out_end(0)
    x_end(0)
    gather_z(0)
    gather_core(1)
    gather_y(0)
    gather_end(1)
    gather_core(0)
    gather_end(0)


def on_device(
    window_input,
    output_cotangent,
    ocean_mask,
    dw_kernel,
    channel_params,
    up_weight,
    up_bias,
    down_weight,
):
    mask = ocean_mask.astype(BF16).reshape(4, N_LAT, COLS).transpose(1, 2, 0).reshape(N_LAT, PART, 1)
    mask = jnp.broadcast_to(mask, (N_LAT, PART, 128))
    taps = jnp.pad(dw_kernel[0].reshape(7, 7, C), ((0, 0), (0, 1), (0, 0))).reshape(56, C)
    params = jnp.pad(channel_params[0], ((0, 3), (0, 0)))
    bias = jnp.pad(up_bias[0].reshape(4, C), ((0, 12), (0, 0)))
    small = jnp.concatenate([taps, params, bias], axis=0)
    vmem = pl.BlockSpec(memory_space=pltpu.VMEM)
    hbm = pl.BlockSpec(memory_space=pl.ANY)
    boundary, gup, gdown, gsmall = pl.pallas_call(
        step_kernel,
        out_shape=(
            jax.ShapeDtypeStruct((2, 4, PART, C), BF16),
            jax.ShapeDtypeStruct((256, 1024), F32),
            jax.ShapeDtypeStruct((1024, 256), F32),
            jax.ShapeDtypeStruct((8, 32, 128), F32),
        ),
        in_specs=[vmem, vmem, vmem, vmem, hbm, hbm],
        out_specs=(vmem, vmem, vmem, vmem),
        scratch_shapes=[
            pltpu.VMEM((2, 256, 1024), BF16),
            pltpu.VMEM((2, 1024, 256), BF16),
            pltpu.VMEM((2, 80, C), BF16),
            pltpu.VMEM((2, 80, C), F32),
            pltpu.VMEM((4, PART, C), BF16),
            pltpu.VMEM((4, PART, C), BF16),
            pltpu.VMEM((4, PART, C), BF16),
            pltpu.VMEM((4, PART, C), BF16),
            pltpu.VMEM((4, PART, 128), BF16),
            pltpu.VMEM((2, 4 * PART, 128), F32),
            pltpu.VMEM((2, CELLS, 128), F32),
            pltpu.VMEM((CELLS, C), F32),
            pltpu.VMEM((CELLS, 128), F32),
            pltpu.VMEM((COLS + 6, 32, C), F32),
            pltpu.VMEM((3, 7, COLS + 6, ROWS, C), F32),
            pltpu.VMEM((4, 2, EDGE, C), BF16),
            pltpu.VMEM((4, 2, EDGE, C), BF16),
            pltpu.VMEM((CELLS, C), F32),
            pltpu.VMEM((2, CELLS, C), F32),
            pltpu.VMEM((2, CELLS, 1), F32),
            pltpu.VMEM((2, CELLS, C), BF16),
            pltpu.VMEM((2, CELLS, 1024), BF16),
            pltpu.VMEM((2, CELLS, 1024), F32),
            pltpu.VMEM((2, CELLS, C), F32),
            pltpu.VMEM((CELLS, C), F32),
            pltpu.VMEM((CELLS, C), BF16),
            pltpu.VMEM((CELLS, C), F32),
            pltpu.VMEM((CELLS, C), F32),
            pltpu.VMEM((2, 8, SLAB, 128), BF16),
            pltpu.VMEM((8, 32, 128), F32),
            pltpu.VMEM((2, 4, SLAB, 128), BF16),
            pltpu.VMEM((2, 4, SLAB, 128), BF16),
            pltpu.VMEM((2, 3, SLAB, 128), BF16),
            pltpu.VMEM((2, 8, 96, 128), BF16),
            pltpu.VMEM((2, 8, 96, 128), BF16),
            pltpu.VMEM((2, 2, 64, 128), BF16),
            pltpu.VMEM((2, 4, 64, 128), BF16),
            pltpu.VMEM((8, SLAB, 128), BF16),
            pltpu.VMEM((2, 4, PART, C), BF16),
            pltpu.VMEM((2, 4, PART, C), BF16),
            pltpu.VMEM((4, PART, C), F32),
            pltpu.SemaphoreType.DMA((2,)),
            pltpu.SemaphoreType.DMA((N_SEM,)),
            pltpu.SemaphoreType.DMA((N_SEM,)),
        ],
        compiler_params=pltpu.CompilerParams(
            collective_id=0, has_side_effects=True, vmem_limit_bytes=56 << 20
        ),
        name="two_blocks",
    )(window_input, output_cotangent, mask, small, up_weight[0], down_weight[0])
    taps = gsmall[:7, :16].reshape(7, 2, 8, 128)[:, :, :7].transpose(0, 2, 1, 3).reshape(1, 49, C)
    chans = gsmall[:2, 24:29].transpose(1, 0, 2).reshape(1, 5, C)
    return (
        boundary[None],
        taps,
        chans,
        gup[None],
        gsmall[:, 16].reshape(1, 1024),
        gdown[None],
    )


def solution(mesh):
    in_specs = (
        P(None, "lat", "lon", None),
        P(None, "lat", "lon", None),
        P("lat", "lon"),
        P("section", None, None),
        P("section", None, None),
        P("section", None, None),
        P("section", None),
        P("section", None, None),
    )
    out_specs = (
        P("section", None, "lat", "lon", None),
        P("section", None, None),
        P("section", None, None),
        P("section", None, None),
        P("section", None),
        P("section", None, None),
    )
    return jax.shard_map(
        on_device, mesh=mesh, in_specs=in_specs, out_specs=out_specs, check_vma=False
    )
```

```python
import functools
import math

import jax
import jax.numpy as jnp
from jax import lax
from jax.experimental import pallas as pl
from jax.experimental.pallas import tpu as pltpu
from jax.sharding import PartitionSpec as P

MESH = pl.DeviceIdType.MESH
F32 = jnp.float32
BF16 = jnp.bfloat16
N_LAT = 4
N_LON = 32
N_Y = 4
N_Z = 8
COLS = 17
ROWS = 16
CELLS = COLS * ROWS
PART = 68
EDGE = 3 * ROWS
C = 256
BIG = 512
SLAB = 528

norm_eps = 1e-06
gelu_scale = 0.7978845608028654
gelu_cubic = 0.044715
factor = 1.0 / math.sqrt(544)
rows_contract = (((0,), (0,)), ((), ()))
cols_contract = (((1,), (1,)), ((), ()))

S_SMALL, S_UP, S_DOWN, S_UPF, S_DOWNF = 0, 1, 2, 3, 4
S_X, S_M, S_C = 5, 8, 11
S_HALO = 14
S_OWN, S_CROSS = 22, 26
S_SUM = 30
L_CORE, L_CORES, L_F, L_FS, L_G, L_Z = 0, 4, 5, 8, 11, 14
L_AZ, L_AG, L_AF, L_AC = 21, 28, 31, 34
N_SUM = 38
N_SEM = S_SUM + 2 * N_SUM
D_UP, D_DOWN, D_X, D_C, D_OUT, D_FULL = 0, 1, 2, 3, 4, 6
N_LOCAL = 10


def step_kernel(
    x_ref, c_ref, m_ref, taps_ref, par_ref, bias_ref, up_ref, down_ref,
    out_ref, sums_ref,
    w_up, w_down, w_sm, w32, sw, m_own,
    a_x, a_c, a_m, g3,
    dense, mask, pad, shifted, edge_out, edge_in,
    u_buf, normed, inv, z_buf, act, slope, branch, e_buf, dm_buf, du_buf, cot,
    slabs, small, r_core, half, r_f, t_all, r_g, u_all, r_z, full,
    o_send,
    local, send, recv,
):
    sec = lax.axis_index("section")
    lat = lax.axis_index("lat")
    lon = lax.axis_index("lon")
    x, core = lat // 2, lat % 2
    y, z = lon // N_Z, lon % N_Z
    ring = 2 * sec + x

    sibling = {"lat": x * 2 + (1 - core)}
    partner = {"section": 1 - sec, "lat": (1 - x) * 2 + core}
    right = {"lat": (lat + 1) % N_LAT, "lon": (lon + (lat + 1) // N_LAT) % N_LON}
    left = {"lat": (lat + 3) % N_LAT, "lon": (lon + N_LON - 1 + (lat + 3) // N_LAT) % N_LON}

    def lat_peer(d):
        return {"lat": (lat + d) % N_LAT}

    def cross_peer(d):
        return {"section": 1 - sec, "lat": (lat + d) % N_LAT}

    def y_peer(d):
        return {"lon": (y + d) % N_Y * N_Z + z}

    def z_peer(d):
        return {"lon": y * N_Z + (z + d) % N_Z}

    def remote(source, target, slot, peer):
        return pltpu.make_async_remote_copy(
            src_ref=source,
            dst_ref=target,
            send_sem=send.at[slot],
            recv_sem=recv.at[slot],
            device_id=peer,
            device_id_type=MESH,
        )

    def push(source, target, slot, peer):
        copy = remote(source, target, slot, peer)
        copy.start()
        return copy

    def placed(xx, yy):
        return {"section": xx // 2, "lat": xx % 2 * 2 + core, "lon": yy * N_Z + z}

    first = y * (1 - core) + ring * core
    second = ring * (1 - core) + y * core

    def first_peer(d):
        return placed((ring + d * core) % 4, (y + d * (1 - core)) % N_Y)

    def second_peer(d):
        return placed((ring + d * (1 - core)) % 4, (y + d * core) % N_Y)

    sw[...] = jnp.zeros_like(sw)
    for p in range(7):
        sw[8 * p : 8 * p + 7, :] = taps_ref[7 * p : 7 * p + 7, :].astype(F32)
    sw[56:61, :] = par_ref[...].astype(F32)
    for i in range(4):
        sw[64 + i : 65 + i, :] = bias_ref[:, 256 * i : 256 * (i + 1)].astype(F32)
    w_sm[sec] = sw[...].astype(BF16)
    m_own[...] = jnp.zeros_like(m_own)
    m_own[0:4, 0:PART] = m_ref[...].astype(F32)

    peers = [lat_peer(d) for d in range(1, 4)] + [cross_peer(d) for d in range(4)] + [left, right]
    peers += [y_peer(d) for d in range(1, N_Y)] + [z_peer(d) for d in range(1, N_Z)]
    barrier = pltpu.get_barrier_semaphore()
    for peer in peers:
        pl.semaphore_signal(barrier, inc=1, device_id=peer, device_id_type=MESH)
    pl.semaphore_wait(barrier, len(peers))

    def strip(ref, b):
        return ref.at[sec, pl.ds(COLS * b, COLS)]

    x_in = [push(strip(x_ref, (lat + d) % 4), a_x.at[lat], S_X + d - 1, lat_peer(d)) for d in range(1, 4)]
    own_x = pltpu.make_async_copy(strip(x_ref, lat), a_x.at[lat], local.at[D_X])
    own_x.start()
    m_in = [push(m_own, a_m.at[lat], S_M + d - 1, lat_peer(d)) for d in range(1, 4)]
    sm_in = push(w_sm.at[sec], w_sm.at[sec], S_SMALL, partner)
    own_up = pltpu.make_async_copy(up_ref, w_up.at[sec], local.at[D_UP])
    own_down = pltpu.make_async_copy(down_ref, w_down.at[sec], local.at[D_DOWN])
    own_c = pltpu.make_async_copy(strip(c_ref, lat), a_c.at[lat], local.at[D_C])
    own_up.start()
    own_down.start()
    up_rows = pl.ds(pl.multiple_of(core * 128, 128), 128)
    down_rows = pl.ds(pl.multiple_of(core * 512, 512), 512)
    up_in = push(up_ref.at[up_rows], w_up.at[sec, up_rows], S_UP, partner)
    down_in = push(down_ref.at[down_rows], w_down.at[sec, down_rows], S_DOWN, partner)
    c_in = [push(strip(c_ref, (lat + d) % 4), a_c.at[lat], S_C + d - 1, lat_peer(d)) for d in range(1, 4)]
    own_c.start()

    a_m[lat] = m_own[...]
    pad[:, 0:8, :] = jnp.zeros((COLS + 6, 8, C), F32)
    pad[:, 24:32, :] = jnp.zeros((COLS + 6, 8, C), F32)
    small[...] = jnp.zeros_like(small)

    def gather(parts, target):
        for a in range(N_LAT):
            g3[:, 4 * a : 4 * a + 4, :] = parts[a].astype(F32)
        target[...] = g3[...].reshape(CELLS, C)

    def gather_mask():
        rows = jnp.concatenate([a_m[a, 0:4, :] for a in range(N_LAT)], axis=0)
        shape = (COLS, ROWS, 128)
        wanted = COLS * lat + lax.broadcasted_iota(jnp.int32, shape, 0)
        picked = jnp.where(lax.broadcasted_iota(jnp.int32, shape, 2) == wanted, rows[None], 0.0)
        value = jnp.sum(picked, axis=-1, keepdims=True)
        mask[...] = jnp.broadcast_to(value, shape).reshape(CELLS, 128)

    def halo_start(field, number):
        edge_out[number, 0] = field[CELLS - EDGE : CELLS, :].astype(BF16)
        edge_out[number, 1] = field[0:EDGE, :].astype(BF16)
        base = S_HALO + 2 * number
        return [
            push(edge_out.at[number, 0], edge_in.at[number, 0], base, right),
            push(edge_out.at[number, 1], edge_in.at[number, 1], base + 1, left),
        ]

    def halo_end(field, copies, number, slot):
        for j in range(COLS):
            pad[3 + j, 8:24, :] = field[ROWS * j : ROWS * (j + 1), :]
        for copy in copies:
            copy.wait()
        for j in range(3):
            rows = slice(ROWS * j, ROWS * (j + 1))
            pad[j, 8:24, :] = edge_in[number, 0, rows, :].astype(F32)
            pad[COLS + 3 + j, 8:24, :] = edge_in[number, 1, rows, :].astype(F32)

        def shift(col, carry):
            for p in range(7):
                shifted[slot, p, col] = pad[col, 5 + p : 21 + p, :]
            return carry

        lax.fori_loop(0, COLS + 6, shift, 0)

    def stencil(slot, k, reverse, target):
        for h in range(2):
            lanes = slice(128 * h, 128 * (h + 1))

            def tap_row(p, acc):
                taps = w32[k, pl.ds(pl.multiple_of(8 * ((6 - p) if reverse else p), 8), 8), lanes]
                for q in range(7):
                    row = 6 - q if reverse else q
                    window = shifted[slot, p, q : q + COLS, :, lanes]
                    acc = acc + window * taps[row : row + 1, :][None]
                return acc

            acc = lax.fori_loop(0, 7, tap_row, jnp.zeros((COLS, ROWS, 128), F32))
            target[:, lanes] = acc.reshape(CELLS, 128)

    def tap_grads(k):
        for h in range(2):
            lanes = slice(128 * h, 128 * (h + 1))

            def tap_row(p, carry):
                grad = du_buf[:, lanes].reshape(COLS, ROWS, 128)
                for q in range(7):
                    window = shifted[k, p, q : q + COLS, :, lanes]
                    total = jnp.sum((grad * window).reshape(CELLS, 128), axis=0, keepdims=True)
                    small[p, 7 * h + q : 7 * h + q + 1, :] = total
                return carry

            lax.fori_loop(0, 7, tap_row, 0)

    def wide_mask():
        return jnp.concatenate([mask[...], mask[...]], axis=1)

    def normalise(k):
        u = u_buf[...] + w32[k, 56:57, :]
        centered = u - jnp.mean(u, axis=-1, keepdims=True)
        inverse = lax.rsqrt(jnp.mean(centered * centered, axis=-1, keepdims=True) + norm_eps)
        value = centered * inverse
        inv[k] = inverse
        normed[k] = value
        z_buf[k] = (value * w32[k, 57:58, :] + w32[k, 58:59, :]).astype(BF16)

    def mlp_hidden(k):
        def chunk(i, carry):
            cols = pl.ds(pl.multiple_of(256 * i, 256), 256)
            hidden = jnp.dot(z_buf[k], w_up[k, :, cols], preferred_element_type=F32)
            hidden = hidden + w32[k, pl.ds(64 + i, 1), :]
            square = hidden * hidden
            tangent = jnp.tanh(gelu_scale * (hidden + gelu_cubic * square * hidden))
            act[k, :, cols] = (0.5 * hidden * (1.0 + tangent)).astype(BF16)
            slope[k, :, cols] = 0.5 * (1.0 + tangent) + 0.5 * hidden * (1.0 - tangent * tangent) * gelu_scale * (
                1.0 + 3.0 * gelu_cubic * square
            )
            return carry

        lax.fori_loop(0, 4, chunk, 0)

    def mlp_out(k, target):
        value = jnp.dot(act[k], w_down[k], preferred_element_type=F32) + w32[k, 59:60, :]
        branch[k] = value
        result = wide_mask() * (dense[...] + w32[k, 60:61, :] * value)
        target[...] = result.astype(BF16).astype(F32)

    def put_small(row, total):
        small[7, row : row + 1, :] = total[:, 0:128]
        small[7, row + 5 : row + 6, :] = total[:, 128:256]

    def mlp_back(k):
        e = wide_mask() * cot[...]
        e_buf[...] = e
        put_small(4, jnp.sum(e * branch[k], axis=0, keepdims=True))
        dm_wide = (w32[k, 60:61, :] * e).astype(BF16)
        dm_buf[...] = dm_wide
        put_small(3, jnp.sum(dm_wide.astype(F32), axis=0, keepdims=True))
        u_buf[...] = jnp.zeros((CELLS, C), F32)

        def chunk(step, carry):
            i = (step + 2 * (1 - core)) % 4
            cols = pl.ds(pl.multiple_of(256 * i, 256), 256)
            dm = dm_buf[...]
            da = lax.dot_general(dm, w_down[k, cols, :], cols_contract, preferred_element_type=F32)
            dh = (da * slope[k, :, cols]).astype(BF16)
            bias = jnp.sum(dh.astype(F32), axis=0, keepdims=True)
            u_buf[...] += lax.dot_general(dh, w_up[k, :, cols], cols_contract, preferred_element_type=F32)
            gup = lax.dot_general(z_buf[k], dh, rows_contract, preferred_element_type=F32).astype(BF16)
            gdown = lax.dot_general(act[k, :, cols], dm, rows_contract, preferred_element_type=F32).astype(BF16)
            for t in range(2):
                slab = 2 * i + t
                cut = slice(128 * t, 128 * (t + 1))
                small[slab, 14:15, :] = bias[:, cut]
                slabs[k, slab, 0:256, :] = gup[:, cut]
                slabs[k, slab, 256:384, :] = gdown[cut, 0:128]
                slabs[k, slab, 384:512, :] = gdown[cut, 128:256]
            return carry

        lax.fori_loop(0, 2, chunk, 0)
        core_big(k)
        lax.fori_loop(2, 4, chunk, 0)
        dz = u_buf[...]
        put_small(1, jnp.sum(dz * normed[k], axis=0, keepdims=True))
        put_small(2, jnp.sum(dz, axis=0, keepdims=True))
        dn = dz * w32[k, 57:58, :]
        first = jnp.mean(dn, axis=-1, keepdims=True)
        second = jnp.mean(dn * normed[k], axis=-1, keepdims=True)
        du = (inv[k] * (dn - first - normed[k] * second)).astype(BF16).astype(F32)
        du_buf[...] = du
        put_small(0, jnp.sum(du, axis=0, keepdims=True))

    other = pl.ds(4 * (1 - core), 4)
    mine4 = 4 * core
    my_slab = mine4 + first

    def sem(k, number):
        return S_SUM + N_SUM * k + number

    def core_copy(k, i):
        return remote(
            slabs.at[k, 4 * (1 - core) + i, pl.ds(0, BIG)], r_core.at[k, i, pl.ds(0, BIG)], sem(k, L_CORE + i), sibling
        )

    def core_big(k):
        for i in range(4):
            core_copy(k, i).start()

    def core_small_copy(k):
        return remote(
            slabs.at[k, other, pl.ds(BIG, 16)], r_core.at[k, :, pl.ds(BIG, 16)], sem(k, L_CORES), sibling
        )

    def core_small(k):
        for slab in range(8):
            slabs[k, slab, BIG:SLAB, :] = small[slab].astype(BF16)
        core_small_copy(k).start()

    def first_add(k, i, rows):
        total = slabs[k, mine4 + i, rows, :].astype(F32) + r_core[k, i, rows, :].astype(F32)
        half[k, i, rows, :] = total.astype(BF16)

    def first_copy(k, d, low, size, number):
        span = pl.ds(low, size)
        return remote(
            half.at[k, (first + d) % 4, span], r_f.at[k, d - 1, span], sem(k, number + d - 1), first_peer(d)
        )

    def first_big(k):
        for i in range(4):
            core_copy(k, i).wait()
        for d in range(1, 4):
            first_add(k, (first + d) % 4, slice(0, BIG))
            first_copy(k, d, 0, BIG, L_F).start()
        first_add(k, first, slice(0, BIG))

    def first_small(k):
        core_small_copy(k).wait()
        for i in range(4):
            first_add(k, i, slice(BIG, SLAB))
        for d in range(1, 4):
            first_copy(k, d, BIG, 16, L_FS).start()

    def second_copy(k, d):
        return remote(t_all.at[k, (second + d) % 4], r_g.at[k, second], sem(k, L_G + d - 1), second_peer(d))

    def second_phase(k):
        for d in range(1, 4):
            first_copy(k, d, 0, BIG, L_F).wait()
            first_copy(k, d, BIG, 16, L_FS).wait()

        def total(rows):
            value = half[k, first, rows, :].astype(F32)
            for d in range(3):
                value = value + r_f[k, d, rows, :].astype(F32)
            return value.astype(BF16)

        tail = total(slice(BIG, SLAB))
        for i in range(4):
            t_all[k, i, 0:128, :] = total(slice(128 * i, 128 * (i + 1)))
            t_all[k, i, 128:144, :] = tail
        for d in range(1, 4):
            second_copy(k, d).start()
        r_g[k, second] = t_all[k, second]

    def z_copy(k, d):
        return remote(u_all.at[k, (z + d) % N_Z], r_z.at[k, z], sem(k, L_Z + d - 1), z_peer(d))

    def z_phase(k):
        for d in range(1, 4):
            second_copy(k, d).wait()
        value = r_g[k, 0].astype(F32)
        for i in range(1, 4):
            value = value + r_g[k, i].astype(F32)
        value = value.astype(BF16)
        for i in range(N_Z):
            u_all[k, i, 0:16, :] = value[16 * i : 16 * (i + 1)]
            u_all[k, i, 16:32, :] = value[128:144]
        for d in range(1, N_Z):
            z_copy(k, d).start()
        r_z[k, z] = u_all[k, z]

    my_rows = pl.ds(pl.multiple_of(128 * second + 16 * z, 16), 16)
    my_group = pl.ds(pl.multiple_of(128 * second, 128), 128)

    def back_z_copy(k, d):
        spot = full.at[k, my_slab, my_rows]
        return remote(spot, spot, sem(k, L_AZ + d - 1), z_peer(d))

    def back_second_copy(k, d):
        spot = full.at[k, my_slab, my_group]
        return remote(spot, spot, sem(k, L_AG + d - 1), second_peer(d))

    def back_first_copy(k, d):
        spot = full.at[k, my_slab]
        return remote(spot, spot, sem(k, L_AF + d - 1), first_peer(d))

    def back_core_copy(k, i):
        spot = full.at[k, mine4 + i]
        return remote(spot, spot, sem(k, L_AC + i), sibling)

    def reached(k, d):
        return (ring + d) % 4 // 2 == k

    def sends_second(k, d):
        return jnp.logical_or(core == 1, reached(k, d))

    def gets_second(k):
        return jnp.logical_or(core == 1, sec == k)

    def sends_first(k, d):
        return jnp.logical_or(jnp.logical_and(core == 0, sec == k), jnp.logical_and(core == 1, reached(k, d)))

    def back_z(k):
        for d in range(1, N_Z):
            z_copy(k, d).wait()
        value = r_z[k, 0].astype(F32)
        for i in range(1, N_Z):
            value = value + r_z[k, i].astype(F32)
        value = value.astype(BF16)
        full[k, my_slab, my_rows, :] = value[0:16]
        full[k, my_slab, BIG:SLAB, :] = value[16:32]
        for d in range(1, N_Z):
            back_z_copy(k, d).start()

    def back_second(k):
        for d in range(1, N_Z):
            back_z_copy(k, d).wait()
        for d in range(1, 4):

            @pl.when(sends_second(k, d))
            def _(d=d):
                back_second_copy(k, d).start()

    def back_first(k):
        for d in range(1, 4):

            @pl.when(sends_second(k, d))
            def _(d=d):
                back_second_copy(k, d).wait_send()

        @pl.when(gets_second(k))
        def _():
            for d in range(1, 4):
                back_second_copy(k, d).wait_recv()

        for d in range(1, 4):

            @pl.when(sends_first(k, d))
            def _(d=d):
                back_first_copy(k, d).start()

    def back_core(k):
        for d in range(1, 4):

            @pl.when(sends_first(k, d))
            def _(d=d):
                back_first_copy(k, d).wait_send()

        @pl.when(sec == k)
        def _():
            for d in range(1, 4):
                back_first_copy(k, d).wait_recv()
            for i in range(4):
                back_core_copy(k, i).start()
            pltpu.make_async_copy(
                full.at[k, pl.ds(mine4, 4)], sums_ref.at[pl.ds(mine4, 4)], local.at[D_FULL]
            ).start()

    def back_end(k):
        @pl.when(sec == k)
        def _():
            for i in range(4):
                back_core_copy(k, i).wait()
            rest = pltpu.make_async_copy(full.at[k, other], sums_ref.at[other], local.at[D_FULL + 1])
            rest.start()
            pltpu.make_async_copy(
                full.at[k, pl.ds(mine4, 4)], sums_ref.at[pl.ds(mine4, 4)], local.at[D_FULL]
            ).wait()
            rest.wait()

    def own_out(k):
        return pltpu.make_async_copy(o_send.at[k, lat], out_ref.at[k, pl.ds(COLS * lat, COLS)], local.at[D_OUT + k])

    def out_copy(k, d, peer, sample, number):
        return remote(
            o_send.at[k, (lat + d) % 4], out_ref.at[sample, pl.ds(COLS * lat, COLS)], number + d, peer
        )

    def out_start(k, field):
        g3[...] = field[...].reshape(COLS, ROWS, C)
        for a in range(N_LAT):
            o_send[k, a] = g3[:, 4 * a : 4 * a + 4, :].astype(BF16)

        @pl.when(sec == k)
        def _():
            own_out(k).start()
            for d in range(1, 4):
                out_copy(k, d, lat_peer(d), k, S_OWN).start()

        @pl.when(sec != k)
        def _():
            for d in range(4):
                out_copy(k, d, cross_peer(d), 1 - k, S_CROSS).start()

    def out_end(k):
        @pl.when(sec == k)
        def _():
            own_out(k).wait()
            for d in range(1, 4):
                out_copy(k, d, lat_peer(d), k, S_OWN).wait()
            for d in range(4):
                out_copy(k, d, cross_peer(d), 1 - k, S_CROSS).wait_recv()

        @pl.when(sec != k)
        def _():
            for d in range(4):
                out_copy(k, d, cross_peer(d), 1 - k, S_CROSS).wait_send()

    own_x.wait()
    for copy in x_in:
        copy.wait()
    gather(a_x, dense)
    copies = halo_start(dense, 0)
    for copy in m_in:
        copy.wait()
    gather_mask()
    sm_in.wait()
    for k in range(2):
        w32[k] = w_sm[k].astype(F32)
    halo_end(dense, copies, 0, 0)
    stencil(0, 0, False, u_buf)
    normalise(0)
    up_in.wait()
    their_up = w_up.at[1 - sec, up_rows]
    up_fwd = push(their_up, their_up, S_UPF, sibling)
    own_up.wait()
    up_fwd.wait()
    mlp_hidden(0)
    down_in.wait()
    their_down = w_down.at[1 - sec, down_rows]
    down_fwd = push(their_down, their_down, S_DOWNF, sibling)
    own_down.wait()
    down_fwd.wait()
    mlp_out(0, cot)
    dense[...] = cot[...]
    copies = halo_start(dense, 1)
    halo_end(dense, copies, 1, 1)
    stencil(1, 1, False, u_buf)
    normalise(1)
    mlp_hidden(1)
    mlp_out(1, cot)
    out_start(1, cot)

    own_c.wait()
    for copy in c_in:
        copy.wait()
    gather(a_c, cot)
    mlp_back(1)
    copies = halo_start(du_buf, 2)
    first_big(1)
    tap_grads(1)
    core_small(1)
    halo_end(du_buf, copies, 2, 2)
    stencil(2, 1, True, u_buf)
    cot[...] = (e_buf[...] + u_buf[...]).astype(BF16).astype(F32)
    first_small(1)

    mlp_back(0)
    copies = halo_start(du_buf, 3)
    first_big(0)
    second_phase(1)
    tap_grads(0)
    core_small(0)
    z_phase(1)
    halo_end(du_buf, copies, 3, 2)
    stencil(2, 0, True, u_buf)
    cot[...] = (e_buf[...] + u_buf[...]).astype(BF16).astype(F32)
    first_small(0)
    out_start(0, cot)
    back_z(1)
    second_phase(0)
    back_second(1)
    z_phase(0)
    back_first(1)
    back_z(0)
    back_core(1)
    back_second(0)
    back_first(0)
    back_end(1)
    out_end(1)
    out_end(0)
    back_core(0)
    back_end(0)


def unpack_kernel(sums, raw, out_ref, gup_ref, gdown_ref, taps_ref, chans_ref, bias_ref, done):
    move = pltpu.make_async_copy(raw, out_ref, done.at[0])
    move.start()

    def put(i, carry):
        cols = pl.ds(pl.multiple_of(128 * i, 128), 128)
        gup_ref[:, cols] = sums[i, 0:256, :].astype(F32) * factor
        gdown_ref[cols, 0:128] = sums[i, 256:384, :].astype(F32) * factor
        gdown_ref[cols, 128:256] = sums[i, 384:512, :].astype(F32) * factor
        return carry

    lax.fori_loop(0, 8, put, 0)
    for i in range(8):
        piece = sums[i, BIG:SLAB, :].astype(F32) * factor
        bias_ref[:, 128 * i : 128 * (i + 1)] = piece[14:15]
        for h in range(2):
            lanes = slice(128 * h, 128 * (h + 1))
            if i < 7:
                for q in range(7):
                    taps_ref[7 * i + q, :, lanes] = piece[7 * h + q : 7 * h + q + 1]
            else:
                for r in range(5):
                    chans_ref[r, :, lanes] = piece[5 * h + r : 5 * h + r + 1]
    move.wait()


def on_device(
    window_input,
    output_cotangent,
    ocean_mask,
    dw_kernel,
    channel_params,
    up_weight,
    up_bias,
    down_weight,
):
    vmem = pl.BlockSpec(memory_space=pltpu.VMEM)
    hbm = pl.BlockSpec(memory_space=pl.ANY)
    raw, sums = pl.pallas_call(
        step_kernel,
        out_shape=(
            jax.ShapeDtypeStruct((2, PART, 4, C), BF16),
            jax.ShapeDtypeStruct((8, SLAB, 128), BF16),
        ),
        in_specs=[hbm, hbm, vmem, vmem, vmem, vmem, hbm, hbm],
        out_specs=(hbm, hbm),
        scratch_shapes=[
            pltpu.VMEM((2, 256, 1024), BF16),
            pltpu.VMEM((2, 1024, 256), BF16),
            pltpu.VMEM((2, 80, C), BF16),
            pltpu.VMEM((2, 80, C), F32),
            pltpu.VMEM((80, C), F32),
            pltpu.VMEM((8, 128), F32),
            pltpu.VMEM((4, COLS, 4, C), BF16),
            pltpu.VMEM((4, COLS, 4, C), BF16),
            pltpu.VMEM((4, 8, 128), F32),
            pltpu.VMEM((COLS, ROWS, C), F32),
            pltpu.VMEM((CELLS, C), F32),
            pltpu.VMEM((CELLS, 128), F32),
            pltpu.VMEM((COLS + 6, 32, C), F32),
            pltpu.VMEM((3, 7, COLS + 6, ROWS, C), F32),
            pltpu.VMEM((4, 2, EDGE, C), BF16),
            pltpu.VMEM((4, 2, EDGE, C), BF16),
            pltpu.VMEM((CELLS, C), F32),
            pltpu.VMEM((2, CELLS, C), F32),
            pltpu.VMEM((2, CELLS, 1), F32),
            pltpu.VMEM((2, CELLS, C), BF16),
            pltpu.VMEM((2, CELLS, 1024), BF16),
            pltpu.VMEM((2, CELLS, 1024), F32),
            pltpu.VMEM((2, CELLS, C), F32),
            pltpu.VMEM((CELLS, C), F32),
            pltpu.VMEM((CELLS, C), BF16),
            pltpu.VMEM((CELLS, C), F32),
            pltpu.VMEM((CELLS, C), F32),
            pltpu.VMEM((2, 8, SLAB, 128), BF16),
            pltpu.VMEM((8, 16, 128), F32),
            pltpu.VMEM((2, 4, SLAB, 128), BF16),
            pltpu.VMEM((2, 4, SLAB, 128), BF16),
            pltpu.VMEM((2, 3, SLAB, 128), BF16),
            pltpu.VMEM((2, 4, 144, 128), BF16),
            pltpu.VMEM((2, 4, 144, 128), BF16),
            pltpu.VMEM((2, 8, 32, 128), BF16),
            pltpu.VMEM((2, 8, 32, 128), BF16),
            pltpu.VMEM((2, 8, SLAB, 128), BF16),
            pltpu.VMEM((2, 4, COLS, 4, C), BF16),
            pltpu.SemaphoreType.DMA((N_LOCAL,)),
            pltpu.SemaphoreType.DMA((N_SEM,)),
            pltpu.SemaphoreType.DMA((N_SEM,)),
        ],
        compiler_params=pltpu.CompilerParams(
            collective_id=0, has_side_effects=True, vmem_limit_bytes=56 << 20
        ),
        name="two_blocks",
    )(
        window_input.transpose(0, 2, 1, 3),
        output_cotangent.transpose(0, 2, 1, 3),
        ocean_mask,
        dw_kernel[0],
        channel_params[0],
        up_bias,
        up_weight[0],
        down_weight[0],
    )
    boundary, gup, gdown, taps, chans, gbias = pl.pallas_call(
        unpack_kernel,
        out_shape=(
            jax.ShapeDtypeStruct((2, PART, 4, C), BF16),
            jax.ShapeDtypeStruct((256, 1024), F32),
            jax.ShapeDtypeStruct((1024, 256), F32),
            jax.ShapeDtypeStruct((49, 1, C), F32),
            jax.ShapeDtypeStruct((5, 1, C), F32),
            jax.ShapeDtypeStruct((1, 1024), F32),
        ),
        in_specs=[vmem, hbm],
        out_specs=(hbm, vmem, vmem, vmem, vmem, vmem),
        scratch_shapes=[pltpu.SemaphoreType.DMA((1,))],
        compiler_params=pltpu.CompilerParams(vmem_limit_bytes=16 << 20),
        name="unpack",
    )(sums, raw)
    return (
        boundary.transpose(0, 2, 1, 3)[None],
        taps.transpose(1, 0, 2),
        chans.transpose(1, 0, 2),
        gup[None],
        gbias,
        gdown[None],
    )


def solution(mesh):
    in_specs = (
        P(None, "lat", "lon", None),
        P(None, "lat", "lon", None),
        P("lat", "lon"),
        P("section", None, None),
        P("section", None, None),
        P("section", None, None),
        P("section", None),
        P("section", None, None),
    )
    out_specs = (
        P("section", None, "lat", "lon", None),
        P("section", None, None),
        P("section", None, None),
        P("section", None, None),
        P("section", None),
        P("section", None, None),
    )
    return jax.shard_map(
        on_device, mesh=mesh, in_specs=in_specs, out_specs=out_specs, check_vma=False
    )
```

```python
import functools
import math

import jax
import jax.numpy as jnp
from jax import lax
from jax.experimental import pallas as pl
from jax.experimental.pallas import tpu as pltpu
from jax.sharding import PartitionSpec as P

MESH = pl.DeviceIdType.MESH
F32 = jnp.float32
BF16 = jnp.bfloat16
N_LAT = 4
N_LON = 32
N_Y = 4
N_Z = 8
COLS = 17
ROWS = 16
CELLS = COLS * ROWS
PART = 68
EDGE = 3 * ROWS
C = 256
BIG = 512
SLAB = 528

norm_eps = 1e-06
gelu_scale = 0.7978845608028654
gelu_cubic = 0.044715
factor = 1.0 / math.sqrt(544)
rows_contract = (((0,), (0,)), ((), ()))
cols_contract = (((1,), (1,)), ((), ()))

S_SMALL, S_UP, S_DOWN, S_UPF, S_DOWNF = 0, 1, 2, 3, 4
S_X, S_M, S_C = 5, 8, 11
S_HALO = 14
S_OWN, S_CROSS = 22, 26
S_SUM = 30
L_CORE, L_CORES, L_F, L_FS, L_G, L_Z = 0, 4, 5, 8, 11, 14
L_AZ, L_AG, L_AF, L_AC = 21, 28, 31, 34
N_SUM = 38
N_SEM = S_SUM + 2 * N_SUM
D_UP, D_DOWN, D_X, D_C, D_OUT, D_FULL = 0, 1, 2, 3, 4, 6
N_LOCAL = 10


def step_kernel(
    x_ref, c_ref, m_ref, taps_ref, par_ref, bias_ref, up_ref, down_ref,
    out_ref, sums_ref,
    w_up, w_down, w_sm, w32, sw, m_own,
    x_own, a_x, a_c, a_m, g3,
    dense, mask, pad, shifted, edge_out, edge_in,
    u_buf, normed, inv, z_buf, act, slope, branch, e_buf, dm_buf, du_buf, cot,
    slabs, small, r_core, half, r_f, t_all, r_g, u_all, r_z, full,
    o_send,
    local, send, recv,
):
    sec = lax.axis_index("section")
    lat = lax.axis_index("lat")
    lon = lax.axis_index("lon")
    x, core = lat // 2, lat % 2
    y, z = lon // N_Z, lon % N_Z
    ring = 2 * sec + x

    sibling = {"lat": x * 2 + (1 - core)}
    partner = {"section": 1 - sec, "lat": (1 - x) * 2 + core}
    right = {"lat": (lat + 1) % N_LAT, "lon": (lon + (lat + 1) // N_LAT) % N_LON}
    left = {"lat": (lat + 3) % N_LAT, "lon": (lon + N_LON - 1 + (lat + 3) // N_LAT) % N_LON}

    def lat_peer(d):
        return {"lat": (lat + d) % N_LAT}

    def cross_peer(d):
        return {"section": 1 - sec, "lat": (lat + d) % N_LAT}

    def y_peer(d):
        return {"lon": (y + d) % N_Y * N_Z + z}

    def z_peer(d):
        return {"lon": y * N_Z + (z + d) % N_Z}

    def remote(source, target, slot, peer):
        return pltpu.make_async_remote_copy(
            src_ref=source,
            dst_ref=target,
            send_sem=send.at[slot],
            recv_sem=recv.at[slot],
            device_id=peer,
            device_id_type=MESH,
        )

    def push(source, target, slot, peer):
        copy = remote(source, target, slot, peer)
        copy.start()
        return copy

    def placed(xx, yy):
        return {"section": xx // 2, "lat": xx % 2 * 2 + core, "lon": yy * N_Z + z}

    first = y * (1 - core) + ring * core
    second = ring * (1 - core) + y * core

    def first_peer(d):
        return placed((ring + d * core) % 4, (y + d * (1 - core)) % N_Y)

    def second_peer(d):
        return placed((ring + d * (1 - core)) % 4, (y + d * core) % N_Y)

    fetch = pltpu.make_async_copy(x_ref.at[sec], x_own, local.at[D_X])
    fetch.start()
    sw[...] = jnp.zeros_like(sw)
    for p in range(7):
        sw[8 * p : 8 * p + 7, :] = taps_ref[7 * p : 7 * p + 7, :].astype(F32)
    sw[56:61, :] = par_ref[...].astype(F32)
    for i in range(4):
        sw[64 + i : 65 + i, :] = bias_ref[:, 256 * i : 256 * (i + 1)].astype(F32)
    w_sm[sec] = sw[...].astype(BF16)
    m_own[...] = jnp.zeros_like(m_own)
    m_own[0:4, 0:PART] = m_ref[...].astype(F32)

    peers = [lat_peer(d) for d in range(1, 4)] + [cross_peer(d) for d in range(4)] + [left, right]
    peers += [y_peer(d) for d in range(1, N_Y)] + [z_peer(d) for d in range(1, N_Z)]
    barrier = pltpu.get_barrier_semaphore()
    for peer in peers:
        pl.semaphore_signal(barrier, inc=1, device_id=peer, device_id_type=MESH)
    pl.semaphore_wait(barrier, len(peers))

    def strip(ref, b):
        return ref.at[sec, pl.ds(COLS * b, COLS)]

    def x_strip(b):
        return x_own.at[pl.ds(COLS * b, COLS)]

    fetch.wait()
    x_in = [push(x_strip((lat + d) % 4), a_x.at[lat], S_X + d - 1, lat_peer(d)) for d in range(1, 4)]
    m_in = [push(m_own, a_m.at[lat], S_M + d - 1, lat_peer(d)) for d in range(1, 4)]
    sm_in = push(w_sm.at[sec], w_sm.at[sec], S_SMALL, partner)
    own_up = pltpu.make_async_copy(up_ref, w_up.at[sec], local.at[D_UP])
    own_down = pltpu.make_async_copy(down_ref, w_down.at[sec], local.at[D_DOWN])
    own_c = pltpu.make_async_copy(strip(c_ref, lat), a_c.at[lat], local.at[D_C])
    own_up.start()
    own_down.start()
    up_rows = pl.ds(pl.multiple_of(core * 128, 128), 128)
    down_rows = pl.ds(pl.multiple_of(core * 512, 512), 512)
    up_in = push(up_ref.at[up_rows], w_up.at[sec, up_rows], S_UP, partner)
    down_in = push(down_ref.at[down_rows], w_down.at[sec, down_rows], S_DOWN, partner)

    a_m[lat] = m_own[...]
    pad[:, 0:8, :] = jnp.zeros((COLS + 6, 8, C), F32)
    pad[:, 24:32, :] = jnp.zeros((COLS + 6, 8, C), F32)
    small[...] = jnp.zeros_like(small)

    def gather(parts, target):
        for a in range(N_LAT):
            g3[:, 4 * a : 4 * a + 4, :] = parts[a].astype(F32)
        target[...] = g3[...].reshape(CELLS, C)

    def gather_mask():
        rows = jnp.concatenate([a_m[a, 0:4, :] for a in range(N_LAT)], axis=0)
        shape = (COLS, ROWS, 128)
        wanted = COLS * lat + lax.broadcasted_iota(jnp.int32, shape, 0)
        picked = jnp.where(lax.broadcasted_iota(jnp.int32, shape, 2) == wanted, rows[None], 0.0)
        value = jnp.sum(picked, axis=-1, keepdims=True)
        mask[...] = jnp.broadcast_to(value, shape).reshape(CELLS, 128)

    def halo_start(field, number):
        edge_out[number, 0] = field[CELLS - EDGE : CELLS, :].astype(BF16)
        edge_out[number, 1] = field[0:EDGE, :].astype(BF16)
        base = S_HALO + 2 * number
        return [
            push(edge_out.at[number, 0], edge_in.at[number, 0], base, right),
            push(edge_out.at[number, 1], edge_in.at[number, 1], base + 1, left),
        ]

    def shift_columns(slot, low, high):
        def shift(col, carry):
            for p in range(7):
                shifted[slot, p, col] = pad[col, 5 + p : 21 + p, :]
            return carry

        lax.fori_loop(low, high, shift, 0)

    def stencil(slot, k, reverse, target, low, count):
        for h in range(2):
            lanes = slice(128 * h, 128 * (h + 1))

            def tap_row(p, acc):
                taps = w32[k, pl.ds(pl.multiple_of(8 * ((6 - p) if reverse else p), 8), 8), lanes]
                for q in range(7):
                    row = 6 - q if reverse else q
                    window = shifted[slot, p, low + q : low + q + count, :, lanes]
                    acc = acc + window * taps[row : row + 1, :][None]
                return acc

            acc = lax.fori_loop(0, 7, tap_row, jnp.zeros((count, ROWS, 128), F32))
            target[ROWS * low : ROWS * (low + count), lanes] = acc.reshape(ROWS * count, 128)

    def inner_columns(field, slot, k, reverse, target):
        for j in range(COLS):
            pad[3 + j, 8:24, :] = field[ROWS * j : ROWS * (j + 1), :]
        shift_columns(slot, 3, COLS + 3)
        stencil(slot, k, reverse, target, 3, COLS - 6)

    def outer_columns(copies, number, slot, k, reverse, target):
        for copy in copies:
            copy.wait()
        for j in range(3):
            rows = slice(ROWS * j, ROWS * (j + 1))
            pad[j, 8:24, :] = edge_in[number, 0, rows, :].astype(F32)
            pad[COLS + 3 + j, 8:24, :] = edge_in[number, 1, rows, :].astype(F32)
        shift_columns(slot, 0, 3)
        shift_columns(slot, COLS + 3, COLS + 6)
        stencil(slot, k, reverse, target, 0, 3)
        stencil(slot, k, reverse, target, COLS - 3, 3)

    def tap_grads(k):
        for h in range(2):
            lanes = slice(128 * h, 128 * (h + 1))

            def tap_row(p, carry):
                grad = du_buf[:, lanes].reshape(COLS, ROWS, 128)
                for q in range(7):
                    window = shifted[k, p, q : q + COLS, :, lanes]
                    total = jnp.sum((grad * window).reshape(CELLS, 128), axis=0, keepdims=True)
                    small[p, 7 * h + q : 7 * h + q + 1, :] = total
                return carry

            lax.fori_loop(0, 7, tap_row, 0)

    def wide_mask():
        return jnp.concatenate([mask[...], mask[...]], axis=1)

    def normalise(k):
        u = u_buf[...] + w32[k, 56:57, :]
        centered = u - jnp.mean(u, axis=-1, keepdims=True)
        inverse = lax.rsqrt(jnp.mean(centered * centered, axis=-1, keepdims=True) + norm_eps)
        value = centered * inverse
        inv[k] = inverse
        normed[k] = value
        z_buf[k] = (value * w32[k, 57:58, :] + w32[k, 58:59, :]).astype(BF16)

    def mlp_hidden(k):
        def chunk(i, carry):
            cols = pl.ds(pl.multiple_of(256 * i, 256), 256)
            hidden = jnp.dot(z_buf[k], w_up[k, :, cols], preferred_element_type=F32)
            hidden = hidden + w32[k, pl.ds(64 + i, 1), :]
            square = hidden * hidden
            tangent = jnp.tanh(gelu_scale * (hidden + gelu_cubic * square * hidden))
            act[k, :, cols] = (0.5 * hidden * (1.0 + tangent)).astype(BF16)
            slope[k, :, cols] = 0.5 * (1.0 + tangent) + 0.5 * hidden * (1.0 - tangent * tangent) * gelu_scale * (
                1.0 + 3.0 * gelu_cubic * square
            )
            return carry

        lax.fori_loop(0, 4, chunk, 0)

    def mlp_out(k, target):
        value = jnp.dot(act[k], w_down[k], preferred_element_type=F32) + w32[k, 59:60, :]
        branch[k] = value
        result = wide_mask() * (dense[...] + w32[k, 60:61, :] * value)
        target[...] = result.astype(BF16).astype(F32)

    def put_small(row, total):
        small[7, row : row + 1, :] = total[:, 0:128]
        small[7, row + 5 : row + 6, :] = total[:, 128:256]

    def mlp_back(k):
        e = wide_mask() * cot[...]
        e_buf[...] = e
        put_small(4, jnp.sum(e * branch[k], axis=0, keepdims=True))
        dm_wide = (w32[k, 60:61, :] * e).astype(BF16)
        dm_buf[...] = dm_wide
        put_small(3, jnp.sum(dm_wide.astype(F32), axis=0, keepdims=True))
        u_buf[...] = jnp.zeros((CELLS, C), F32)

        def chunk(step, carry):
            i = (step + 2 * (1 - core)) % 4
            cols = pl.ds(pl.multiple_of(256 * i, 256), 256)
            dm = dm_buf[...]
            da = lax.dot_general(dm, w_down[k, cols, :], cols_contract, preferred_element_type=F32)
            dh = (da * slope[k, :, cols]).astype(BF16)
            bias = jnp.sum(dh.astype(F32), axis=0, keepdims=True)
            u_buf[...] += lax.dot_general(dh, w_up[k, :, cols], cols_contract, preferred_element_type=F32)
            gup = lax.dot_general(z_buf[k], dh, rows_contract, preferred_element_type=F32).astype(BF16)
            gdown = lax.dot_general(act[k, :, cols], dm, rows_contract, preferred_element_type=F32).astype(BF16)
            for t in range(2):
                slab = 2 * i + t
                cut = slice(128 * t, 128 * (t + 1))
                small[slab, 14:15, :] = bias[:, cut]
                slabs[k, slab, 0:256, :] = gup[:, cut]
                slabs[k, slab, 256:384, :] = gdown[cut, 0:128]
                slabs[k, slab, 384:512, :] = gdown[cut, 128:256]
            return carry

        lax.fori_loop(0, 2, chunk, 0)
        core_big(k)
        lax.fori_loop(2, 4, chunk, 0)
        dz = u_buf[...]
        put_small(1, jnp.sum(dz * normed[k], axis=0, keepdims=True))
        put_small(2, jnp.sum(dz, axis=0, keepdims=True))
        dn = dz * w32[k, 57:58, :]
        first = jnp.mean(dn, axis=-1, keepdims=True)
        second = jnp.mean(dn * normed[k], axis=-1, keepdims=True)
        du = (inv[k] * (dn - first - normed[k] * second)).astype(BF16).astype(F32)
        du_buf[...] = du
        put_small(0, jnp.sum(du, axis=0, keepdims=True))

    other = pl.ds(4 * (1 - core), 4)
    mine4 = 4 * core
    my_slab = mine4 + first

    def sem(k, number):
        return S_SUM + N_SUM * k + number

    def core_copy(k, i):
        return remote(
            slabs.at[k, 4 * (1 - core) + i, pl.ds(0, BIG)], r_core.at[k, i, pl.ds(0, BIG)], sem(k, L_CORE + i), sibling
        )

    def core_big(k):
        for i in range(4):
            core_copy(k, i).start()

    def core_small_copy(k):
        return remote(
            slabs.at[k, other, pl.ds(BIG, 16)], r_core.at[k, :, pl.ds(BIG, 16)], sem(k, L_CORES), sibling
        )

    def core_small(k):
        for slab in range(8):
            slabs[k, slab, BIG:SLAB, :] = small[slab].astype(BF16)
        core_small_copy(k).start()

    def first_add(k, i, rows):
        total = slabs[k, mine4 + i, rows, :].astype(F32) + r_core[k, i, rows, :].astype(F32)
        half[k, i, rows, :] = total.astype(BF16)

    def first_copy(k, d, low, size, number):
        span = pl.ds(low, size)
        return remote(
            half.at[k, (first + d) % 4, span], r_f.at[k, d - 1, span], sem(k, number + d - 1), first_peer(d)
        )

    def first_big(k):
        for i in range(4):
            core_copy(k, i).wait()
        for d in range(1, 4):
            first_add(k, (first + d) % 4, slice(0, BIG))
            first_copy(k, d, 0, BIG, L_F).start()
        first_add(k, first, slice(0, BIG))

    def first_small(k):
        core_small_copy(k).wait()
        for i in range(4):
            first_add(k, i, slice(BIG, SLAB))
        for d in range(1, 4):
            first_copy(k, d, BIG, 16, L_FS).start()

    def second_copy(k, d):
        return remote(t_all.at[k, (second + d) % 4], r_g.at[k, second], sem(k, L_G + d - 1), second_peer(d))

    def second_phase(k):
        for d in range(1, 4):
            first_copy(k, d, 0, BIG, L_F).wait()
            first_copy(k, d, BIG, 16, L_FS).wait()

        def total(rows):
            value = half[k, first, rows, :].astype(F32)
            for d in range(3):
                value = value + r_f[k, d, rows, :].astype(F32)
            return value.astype(BF16)

        tail = total(slice(BIG, SLAB))
        for i in range(4):
            t_all[k, i, 0:128, :] = total(slice(128 * i, 128 * (i + 1)))
            t_all[k, i, 128:144, :] = tail
        for d in range(1, 4):
            second_copy(k, d).start()
        r_g[k, second] = t_all[k, second]

    def z_copy(k, d):
        return remote(u_all.at[k, (z + d) % N_Z], r_z.at[k, z], sem(k, L_Z + d - 1), z_peer(d))

    def z_phase(k):
        for d in range(1, 4):
            second_copy(k, d).wait()
        value = r_g[k, 0].astype(F32)
        for i in range(1, 4):
            value = value + r_g[k, i].astype(F32)
        value = value.astype(BF16)
        for i in range(N_Z):
            u_all[k, i, 0:16, :] = value[16 * i : 16 * (i + 1)]
            u_all[k, i, 16:32, :] = value[128:144]
        for d in range(1, N_Z):
            z_copy(k, d).start()
        r_z[k, z] = u_all[k, z]

    my_rows = pl.ds(pl.multiple_of(128 * second + 16 * z, 16), 16)
    my_group = pl.ds(pl.multiple_of(128 * second, 128), 128)

    def back_z_copy(k, d):
        spot = full.at[k, my_slab, my_rows]
        return remote(spot, spot, sem(k, L_AZ + d - 1), z_peer(d))

    def back_second_copy(k, d):
        spot = full.at[k, my_slab, my_group]
        return remote(spot, spot, sem(k, L_AG + d - 1), second_peer(d))

    def back_first_copy(k, d):
        spot = full.at[k, my_slab]
        return remote(spot, spot, sem(k, L_AF + d - 1), first_peer(d))

    def back_core_copy(k, d):
        spot = full.at[k, mine4 + (first + 4 - d) % 4]
        return remote(spot, spot, sem(k, L_AC + d), sibling)

    def reached(k, d):
        return (ring + d) % 4 // 2 == k

    def sends_second(k, d):
        return jnp.logical_or(core == 1, reached(k, d))

    def gets_second(k):
        return jnp.logical_or(core == 1, sec == k)

    def sends_first(k, d):
        return jnp.logical_or(jnp.logical_and(core == 0, sec == k), jnp.logical_and(core == 1, reached(k, d)))

    def back_z(k):
        for d in range(1, N_Z):
            z_copy(k, d).wait()
        value = r_z[k, 0].astype(F32)
        for i in range(1, N_Z):
            value = value + r_z[k, i].astype(F32)
        value = value.astype(BF16)
        full[k, my_slab, my_rows, :] = value[0:16]
        full[k, my_slab, BIG:SLAB, :] = value[16:32]
        for d in range(1, N_Z):
            back_z_copy(k, d).start()

    def back_second(k):
        for d in range(1, N_Z):
            back_z_copy(k, d).wait()
        for d in range(1, 4):

            @pl.when(sends_second(k, d))
            def _(d=d):
                back_second_copy(k, d).start()

    def back_first(k):
        for d in range(1, 4):

            @pl.when(sends_second(k, d))
            def _(d=d):
                back_second_copy(k, d).wait_send()

        @pl.when(gets_second(k))
        def _():
            for d in range(1, 4):
                back_second_copy(k, d).wait_recv()

        for d in range(1, 4):

            @pl.when(sends_first(k, d))
            def _(d=d):
                back_first_copy(k, d).start()

    def back_core(k):
        @pl.when(sec == k)
        def _():
            back_core_copy(k, 0).start()
            for d in range(1, 4):
                back_first_copy(k, d).wait_recv()
                back_core_copy(k, d).start()
            pltpu.make_async_copy(
                full.at[k, pl.ds(mine4, 4)], sums_ref.at[pl.ds(mine4, 4)], local.at[D_FULL]
            ).start()

        for d in range(1, 4):

            @pl.when(sends_first(k, d))
            def _(d=d):
                back_first_copy(k, d).wait_send()

    def back_end(k):
        @pl.when(sec == k)
        def _():
            for i in range(4):
                back_core_copy(k, i).wait()
            rest = pltpu.make_async_copy(full.at[k, other], sums_ref.at[other], local.at[D_FULL + 1])
            rest.start()
            pltpu.make_async_copy(
                full.at[k, pl.ds(mine4, 4)], sums_ref.at[pl.ds(mine4, 4)], local.at[D_FULL]
            ).wait()
            rest.wait()

    def own_out(k):
        return pltpu.make_async_copy(o_send.at[k, lat], out_ref.at[k, pl.ds(COLS * lat, COLS)], local.at[D_OUT + k])

    def out_copy(k, d, peer, sample, number):
        return remote(
            o_send.at[k, (lat + d) % 4], out_ref.at[sample, pl.ds(COLS * lat, COLS)], number + d, peer
        )

    def out_start(k, field):
        g3[...] = field[...].reshape(COLS, ROWS, C)
        for a in range(N_LAT):
            o_send[k, a] = g3[:, 4 * a : 4 * a + 4, :].astype(BF16)

        @pl.when(sec == k)
        def _():
            own_out(k).start()
            for d in range(1, 4):
                out_copy(k, d, lat_peer(d), k, S_OWN).start()

        @pl.when(sec != k)
        def _():
            for d in range(4):
                out_copy(k, d, cross_peer(d), 1 - k, S_CROSS).start()

    def out_end(k):
        @pl.when(sec == k)
        def _():
            own_out(k).wait()
            for d in range(1, 4):
                out_copy(k, d, lat_peer(d), k, S_OWN).wait()
            for d in range(4):
                out_copy(k, d, cross_peer(d), 1 - k, S_CROSS).wait_recv()

        @pl.when(sec != k)
        def _():
            for d in range(4):
                out_copy(k, d, cross_peer(d), 1 - k, S_CROSS).wait_send()

    a_x[lat] = x_own[pl.ds(COLS * lat, COLS)]
    for copy in x_in:
        copy.wait()
    gather(a_x, dense)
    copies = halo_start(dense, 0)
    for copy in m_in:
        copy.wait()
    gather_mask()
    sm_in.wait()
    for k in range(2):
        w32[k] = w_sm[k].astype(F32)
    inner_columns(dense, 0, 0, False, u_buf)
    outer_columns(copies, 0, 0, 0, False, u_buf)
    normalise(0)
    up_in.wait()
    their_up = w_up.at[1 - sec, up_rows]
    up_fwd = push(their_up, their_up, S_UPF, sibling)
    own_up.wait()
    up_fwd.wait()
    mlp_hidden(0)
    down_in.wait()
    their_down = w_down.at[1 - sec, down_rows]
    down_fwd = push(their_down, their_down, S_DOWNF, sibling)
    own_down.wait()
    down_fwd.wait()
    mlp_out(0, cot)
    dense[...] = cot[...]
    copies = halo_start(dense, 1)
    c_in = [push(strip(c_ref, (lat + d) % 4), a_c.at[lat], S_C + d - 1, lat_peer(d)) for d in range(1, 4)]
    own_c.start()
    inner_columns(dense, 1, 1, False, u_buf)
    outer_columns(copies, 1, 1, 1, False, u_buf)
    normalise(1)
    mlp_hidden(1)
    mlp_out(1, cot)
    out_start(1, cot)

    own_c.wait()
    for copy in c_in:
        copy.wait()
    gather(a_c, cot)
    mlp_back(1)
    copies = halo_start(du_buf, 2)
    first_big(1)
    tap_grads(1)
    core_small(1)
    inner_columns(du_buf, 2, 1, True, u_buf)
    outer_columns(copies, 2, 2, 1, True, u_buf)
    cot[...] = (e_buf[...] + u_buf[...]).astype(BF16).astype(F32)
    first_small(1)

    mlp_back(0)
    copies = halo_start(du_buf, 3)
    first_big(0)
    tap_grads(0)
    core_small(0)
    second_phase(1)
    first_small(0)
    z_phase(1)
    inner_columns(du_buf, 2, 0, True, u_buf)
    second_phase(0)
    outer_columns(copies, 3, 2, 0, True, u_buf)
    z_phase(0)
    cot[...] = (e_buf[...] + u_buf[...]).astype(BF16).astype(F32)
    out_start(0, cot)
    back_z(1)
    back_z(0)
    back_second(1)
    back_second(0)
    back_first(1)
    back_first(0)
    back_core(1)
    back_core(0)
    out_end(1)
    out_end(0)
    back_end(1)
    back_end(0)


def unpack_kernel(
    sums, raw, out_ref, gup_ref, gdown_ref, taps_ref, chans_ref, bias_ref, held, raw_held, wide, tall, done
):
    loads = [pltpu.make_async_copy(sums.at[i], held.at[i], done.at[i]) for i in range(8)]
    raw_in = pltpu.make_async_copy(raw, raw_held, done.at[24])
    raw_out = pltpu.make_async_copy(raw_held, out_ref, done.at[25])
    for load in loads[:2]:
        load.start()
    raw_in.start()
    for load in loads[2:]:
        load.start()
    stores = []
    for i in range(8):
        loads[i].wait()
        cols = pl.ds(128 * i, 128)
        wide[i] = held[i, 0:256, :].astype(F32) * factor
        tall[i, :, 0:128] = held[i, 256:384, :].astype(F32) * factor
        tall[i, :, 128:256] = held[i, 384:512, :].astype(F32) * factor
        stores.append(pltpu.make_async_copy(wide.at[i], gup_ref.at[:, cols], done.at[8 + i]))
        stores.append(pltpu.make_async_copy(tall.at[i], gdown_ref.at[cols], done.at[16 + i]))
        stores[-2].start()
        stores[-1].start()
        if i == 2:
            raw_in.wait()
            raw_out.start()
        piece = held[i, BIG:SLAB, :].astype(F32) * factor
        bias_ref[:, 128 * i : 128 * (i + 1)] = piece[14:15]
        for h in range(2):
            lanes = slice(128 * h, 128 * (h + 1))
            if i < 7:
                for q in range(7):
                    taps_ref[7 * i + q, :, lanes] = piece[7 * h + q : 7 * h + q + 1]
            else:
                for r in range(5):
                    chans_ref[r, :, lanes] = piece[5 * h + r : 5 * h + r + 1]
    raw_out.wait()
    for store in stores:
        store.wait()


def on_device(
    window_input,
    output_cotangent,
    ocean_mask,
    dw_kernel,
    channel_params,
    up_weight,
    up_bias,
    down_weight,
):
    vmem = pl.BlockSpec(memory_space=pltpu.VMEM)
    hbm = pl.BlockSpec(memory_space=pl.ANY)
    raw, sums = pl.pallas_call(
        step_kernel,
        out_shape=(
            jax.ShapeDtypeStruct((2, PART, 4, C), BF16),
            jax.ShapeDtypeStruct((8, SLAB, 128), BF16),
        ),
        in_specs=[hbm, hbm, vmem, vmem, vmem, vmem, hbm, hbm],
        out_specs=(hbm, hbm),
        scratch_shapes=[
            pltpu.VMEM((2, 256, 1024), BF16),
            pltpu.VMEM((2, 1024, 256), BF16),
            pltpu.VMEM((2, 80, C), BF16),
            pltpu.VMEM((2, 80, C), F32),
            pltpu.VMEM((80, C), F32),
            pltpu.VMEM((8, 128), F32),
            pltpu.VMEM((PART, 4, C), BF16),
            pltpu.VMEM((4, COLS, 4, C), BF16),
            pltpu.VMEM((4, COLS, 4, C), BF16),
            pltpu.VMEM((4, 8, 128), F32),
            pltpu.VMEM((COLS, ROWS, C), F32),
            pltpu.VMEM((CELLS, C), F32),
            pltpu.VMEM((CELLS, 128), F32),
            pltpu.VMEM((COLS + 6, 32, C), F32),
            pltpu.VMEM((3, 7, COLS + 6, ROWS, C), F32),
            pltpu.VMEM((4, 2, EDGE, C), BF16),
            pltpu.VMEM((4, 2, EDGE, C), BF16),
            pltpu.VMEM((CELLS, C), F32),
            pltpu.VMEM((2, CELLS, C), F32),
            pltpu.VMEM((2, CELLS, 1), F32),
            pltpu.VMEM((2, CELLS, C), BF16),
            pltpu.VMEM((2, CELLS, 1024), BF16),
            pltpu.VMEM((2, CELLS, 1024), F32),
            pltpu.VMEM((2, CELLS, C), F32),
            pltpu.VMEM((CELLS, C), F32),
            pltpu.VMEM((CELLS, C), BF16),
            pltpu.VMEM((CELLS, C), F32),
            pltpu.VMEM((CELLS, C), F32),
            pltpu.VMEM((2, 8, SLAB, 128), BF16),
            pltpu.VMEM((8, 16, 128), F32),
            pltpu.VMEM((2, 4, SLAB, 128), BF16),
            pltpu.VMEM((2, 4, SLAB, 128), BF16),
            pltpu.VMEM((2, 3, SLAB, 128), BF16),
            pltpu.VMEM((2, 4, 144, 128), BF16),
            pltpu.VMEM((2, 4, 144, 128), BF16),
            pltpu.VMEM((2, 8, 32, 128), BF16),
            pltpu.VMEM((2, 8, 32, 128), BF16),
            pltpu.VMEM((2, 8, SLAB, 128), BF16),
            pltpu.VMEM((2, 4, COLS, 4, C), BF16),
            pltpu.SemaphoreType.DMA((N_LOCAL,)),
            pltpu.SemaphoreType.DMA((N_SEM,)),
            pltpu.SemaphoreType.DMA((N_SEM,)),
        ],
        compiler_params=pltpu.CompilerParams(
            collective_id=0, has_side_effects=True, vmem_limit_bytes=56 << 20
        ),
        name="two_blocks",
    )(
        window_input.transpose(0, 2, 1, 3),
        output_cotangent.transpose(0, 2, 1, 3),
        ocean_mask,
        dw_kernel[0],
        channel_params[0],
        up_bias,
        up_weight[0],
        down_weight[0],
    )
    boundary, gup, gdown, taps, chans, gbias = pl.pallas_call(
        unpack_kernel,
        out_shape=(
            jax.ShapeDtypeStruct((2, PART, 4, C), BF16),
            jax.ShapeDtypeStruct((256, 1024), F32),
            jax.ShapeDtypeStruct((1024, 256), F32),
            jax.ShapeDtypeStruct((49, 1, C), F32),
            jax.ShapeDtypeStruct((5, 1, C), F32),
            jax.ShapeDtypeStruct((1, 1024), F32),
        ),
        in_specs=[hbm, hbm],
        out_specs=(hbm, hbm, hbm, vmem, vmem, vmem),
        scratch_shapes=[
            pltpu.VMEM((8, SLAB, 128), BF16),
            pltpu.VMEM((2, PART, 4, C), BF16),
            pltpu.VMEM((8, 256, 128), F32),
            pltpu.VMEM((8, 128, 256), F32),
            pltpu.SemaphoreType.DMA((26,)),
        ],
        compiler_params=pltpu.CompilerParams(vmem_limit_bytes=60 << 20),
        name="unpack",
    )(sums, raw)
    return (
        boundary.transpose(0, 2, 1, 3)[None],
        taps.transpose(1, 0, 2),
        chans.transpose(1, 0, 2),
        gup[None],
        gbias,
        gdown[None],
    )


def solution(mesh):
    in_specs = (
        P(None, "lat", "lon", None),
        P(None, "lat", "lon", None),
        P("lat", "lon"),
        P("section", None, None),
        P("section", None, None),
        P("section", None, None),
        P("section", None),
        P("section", None, None),
    )
    out_specs = (
        P("section", None, "lat", "lon", None),
        P("section", None, None),
        P("section", None, None),
        P("section", None, None),
        P("section", None),
        P("section", None, None),
    )
    return jax.shard_map(
        on_device, mesh=mesh, in_specs=in_specs, out_specs=out_specs, check_vma=False
    )
```

```python
import functools
import math

import jax
import jax.numpy as jnp
from jax import lax
from jax.experimental import pallas as pl
from jax.experimental.pallas import tpu as pltpu
from jax.sharding import PartitionSpec as P

MESH = pl.DeviceIdType.MESH
F32 = jnp.float32
BF16 = jnp.bfloat16
N_LAT = 4
N_LON = 32
N_Y = 4
N_Z = 8
COLS = 17
ROWS = 16
CELLS = COLS * ROWS
PART = 68
EDGE = 3 * ROWS
C = 256
BIG = 512
SLAB = 528

norm_eps = 1e-06
gelu_scale = 0.7978845608028654
gelu_cubic = 0.044715
factor = 1.0 / math.sqrt(544)
rows_contract = (((0,), (0,)), ((), ()))
cols_contract = (((1,), (1,)), ((), ()))

S_SMALL, S_UP, S_DOWN, S_UPF, S_DOWNF = 0, 1, 2, 3, 4
S_X, S_M, S_C = 5, 8, 11
S_HALO = 14
S_OWN, S_CROSS = 22, 26
S_SUM = 30
L_CORE, L_CORES, L_F, L_FS, L_G, L_Z = 0, 4, 5, 8, 11, 14
L_AZ, L_AP, L_AC = 21, 28, 43
N_SUM = 59
N_SEM = S_SUM + 2 * N_SUM
D_UP, D_DOWN, D_X, D_C, D_OUT, D_FULL = 0, 1, 2, 3, 4, 6
N_LOCAL = 10


def step_kernel(
    x_ref, c_ref, m_ref, taps_ref, par_ref, bias_ref, up_ref, down_ref,
    out_ref, sums_ref,
    w_up, w_down, w_sm, w32, sw, m_own,
    x_own, a_x, a_c, a_m, g3,
    dense, mask, pad, shifted, edge_out, edge_in,
    u_buf, normed, inv, z_buf, act, slope, branch, e_buf, dm_buf, du_buf, cot,
    slabs, small, r_core, half, r_f, t_all, r_g, u_all, r_z, full,
    o_send,
    local, send, recv,
):
    sec = lax.axis_index("section")
    lat = lax.axis_index("lat")
    lon = lax.axis_index("lon")
    x, core = lat // 2, lat % 2
    y, z = lon // N_Z, lon % N_Z
    ring = 2 * sec + x

    sibling = {"lat": x * 2 + (1 - core)}
    partner = {"section": 1 - sec, "lat": (1 - x) * 2 + core}
    right = {"lat": (lat + 1) % N_LAT, "lon": (lon + (lat + 1) // N_LAT) % N_LON}
    left = {"lat": (lat + 3) % N_LAT, "lon": (lon + N_LON - 1 + (lat + 3) // N_LAT) % N_LON}

    def lat_peer(d):
        return {"lat": (lat + d) % N_LAT}

    def cross_peer(d):
        return {"section": 1 - sec, "lat": (lat + d) % N_LAT}

    def y_peer(d):
        return {"lon": (y + d) % N_Y * N_Z + z}

    def z_peer(d):
        return {"lon": y * N_Z + (z + d) % N_Z}

    def remote(source, target, slot, peer):
        return pltpu.make_async_remote_copy(
            src_ref=source,
            dst_ref=target,
            send_sem=send.at[slot],
            recv_sem=recv.at[slot],
            device_id=peer,
            device_id_type=MESH,
        )

    def push(source, target, slot, peer):
        copy = remote(source, target, slot, peer)
        copy.start()
        return copy

    def placed(xx, yy):
        return {"section": xx // 2, "lat": xx % 2 * 2 + core, "lon": yy * N_Z + z}

    first = y * (1 - core) + ring * core
    second = ring * (1 - core) + y * core

    def first_peer(d):
        return placed((ring + d * core) % 4, (y + d * (1 - core)) % N_Y)

    def second_peer(d):
        return placed((ring + d * (1 - core)) % 4, (y + d * core) % N_Y)

    fetch = pltpu.make_async_copy(x_ref.at[sec], x_own, local.at[D_X])
    fetch.start()
    sw[...] = jnp.zeros_like(sw)
    for p in range(7):
        sw[8 * p : 8 * p + 7, :] = taps_ref[7 * p : 7 * p + 7, :].astype(F32)
    sw[56:61, :] = par_ref[...].astype(F32)
    for i in range(4):
        sw[64 + i : 65 + i, :] = bias_ref[:, 256 * i : 256 * (i + 1)].astype(F32)
    w_sm[sec] = sw[...].astype(BF16)
    m_own[...] = jnp.zeros_like(m_own)
    m_own[0:4, 0:PART] = m_ref[...].astype(F32)

    peers = [lat_peer(d) for d in range(1, 4)] + [cross_peer(d) for d in range(4)] + [left, right]
    peers += [placed((ring + dx) % 4, (y + dy) % N_Y) for dx in range(4) for dy in range(1, N_Y)]
    peers += [z_peer(d) for d in range(1, N_Z)]
    barrier = pltpu.get_barrier_semaphore()
    for peer in peers:
        pl.semaphore_signal(barrier, inc=1, device_id=peer, device_id_type=MESH)
    pl.semaphore_wait(barrier, len(peers))

    def strip(ref, b):
        return ref.at[sec, pl.ds(COLS * b, COLS)]

    def x_strip(b):
        return x_own.at[pl.ds(COLS * b, COLS)]

    fetch.wait()
    x_in = [push(x_strip((lat + d) % 4), a_x.at[lat], S_X + d - 1, lat_peer(d)) for d in range(1, 4)]
    m_in = [push(m_own, a_m.at[lat], S_M + d - 1, lat_peer(d)) for d in range(1, 4)]
    sm_in = push(w_sm.at[sec], w_sm.at[sec], S_SMALL, partner)
    own_up = pltpu.make_async_copy(up_ref, w_up.at[sec], local.at[D_UP])
    own_down = pltpu.make_async_copy(down_ref, w_down.at[sec], local.at[D_DOWN])
    own_c = pltpu.make_async_copy(strip(c_ref, lat), a_c.at[lat], local.at[D_C])
    own_up.start()
    own_down.start()
    up_cols = pl.ds(pl.multiple_of(core * 512, 512), 512)
    down_rows = pl.ds(pl.multiple_of(core * 512, 512), 512)
    up_in = push(up_ref.at[:, up_cols], w_up.at[sec, :, up_cols], S_UP, partner)
    down_in = push(down_ref.at[down_rows], w_down.at[sec, down_rows], S_DOWN, partner)

    a_m[lat] = m_own[...]
    pad[:, 0:8, :] = jnp.zeros((COLS + 6, 8, C), F32)
    pad[:, 24:32, :] = jnp.zeros((COLS + 6, 8, C), F32)
    small[...] = jnp.zeros_like(small)

    def gather(parts, target):
        for a in range(N_LAT):
            g3[:, 4 * a : 4 * a + 4, :] = parts[a].astype(F32)
        target[...] = g3[...].reshape(CELLS, C)

    def gather_mask():
        rows = jnp.concatenate([a_m[a, 0:4, :] for a in range(N_LAT)], axis=0)
        shape = (COLS, ROWS, 128)
        wanted = COLS * lat + lax.broadcasted_iota(jnp.int32, shape, 0)
        picked = jnp.where(lax.broadcasted_iota(jnp.int32, shape, 2) == wanted, rows[None], 0.0)
        value = jnp.sum(picked, axis=-1, keepdims=True)
        mask[...] = jnp.broadcast_to(value, shape).reshape(CELLS, 128)

    def halo_start(field, number):
        edge_out[number, 0] = field[CELLS - EDGE : CELLS, :].astype(BF16)
        edge_out[number, 1] = field[0:EDGE, :].astype(BF16)
        base = S_HALO + 2 * number
        return [
            push(edge_out.at[number, 0], edge_in.at[number, 0], base, right),
            push(edge_out.at[number, 1], edge_in.at[number, 1], base + 1, left),
        ]

    def shift_columns(slot, low, high):
        def shift(col, carry):
            for p in range(7):
                shifted[slot, p, col] = pad[col, 5 + p : 21 + p, :]
            return carry

        lax.fori_loop(low, high, shift, 0)

    def stencil(slot, k, reverse, target, low, count):
        for h in range(2):
            lanes = slice(128 * h, 128 * (h + 1))

            def tap_row(p, acc):
                taps = w32[k, pl.ds(pl.multiple_of(8 * ((6 - p) if reverse else p), 8), 8), lanes]
                for q in range(7):
                    row = 6 - q if reverse else q
                    window = shifted[slot, p, low + q : low + q + count, :, lanes]
                    acc = acc + window * taps[row : row + 1, :][None]
                return acc

            acc = lax.fori_loop(0, 7, tap_row, jnp.zeros((count, ROWS, 128), F32))
            target[ROWS * low : ROWS * (low + count), lanes] = acc.reshape(ROWS * count, 128)

    def inner_columns(field, slot, k, reverse, target):
        for j in range(COLS):
            pad[3 + j, 8:24, :] = field[ROWS * j : ROWS * (j + 1), :]
        shift_columns(slot, 3, COLS + 3)
        stencil(slot, k, reverse, target, 3, COLS - 6)

    def outer_columns(copies, number, slot, k, reverse, target):
        for copy in copies:
            copy.wait()
        for j in range(3):
            rows = slice(ROWS * j, ROWS * (j + 1))
            pad[j, 8:24, :] = edge_in[number, 0, rows, :].astype(F32)
            pad[COLS + 3 + j, 8:24, :] = edge_in[number, 1, rows, :].astype(F32)
        shift_columns(slot, 0, 3)
        shift_columns(slot, COLS + 3, COLS + 6)
        stencil(slot, k, reverse, target, 0, 3)
        stencil(slot, k, reverse, target, COLS - 3, 3)

    def tap_grads(k):
        for h in range(2):
            lanes = slice(128 * h, 128 * (h + 1))

            def tap_row(p, carry):
                grad = du_buf[:, lanes].reshape(COLS, ROWS, 128)
                for q in range(7):
                    window = shifted[k, p, q : q + COLS, :, lanes]
                    total = jnp.sum((grad * window).reshape(CELLS, 128), axis=0, keepdims=True)
                    small[p, 7 * h + q : 7 * h + q + 1, :] = total
                return carry

            lax.fori_loop(0, 7, tap_row, 0)

    def wide_mask():
        return jnp.concatenate([mask[...], mask[...]], axis=1)

    def normalise(k):
        u = u_buf[...] + w32[k, 56:57, :]
        centered = u - jnp.mean(u, axis=-1, keepdims=True)
        inverse = lax.rsqrt(jnp.mean(centered * centered, axis=-1, keepdims=True) + norm_eps)
        value = centered * inverse
        inv[k] = inverse
        normed[k] = value
        z_buf[k] = (value * w32[k, 57:58, :] + w32[k, 58:59, :]).astype(BF16)

    def mlp_hidden(k, low, high):
        def chunk(step, carry):
            i = (step + 2 * core) % 4
            cols = pl.ds(pl.multiple_of(256 * i, 256), 256)
            hidden = jnp.dot(z_buf[k], w_up[k, :, cols], preferred_element_type=F32)
            hidden = hidden + w32[k, pl.ds(64 + i, 1), :]
            square = hidden * hidden
            tangent = jnp.tanh(gelu_scale * (hidden + gelu_cubic * square * hidden))
            act[k, :, cols] = (0.5 * hidden * (1.0 + tangent)).astype(BF16)
            slope[k, :, cols] = 0.5 * (1.0 + tangent) + 0.5 * hidden * (1.0 - tangent * tangent) * gelu_scale * (
                1.0 + 3.0 * gelu_cubic * square
            )
            return carry

        lax.fori_loop(low, high, chunk, 0)

    def mlp_half(k, which):
        units = pl.ds(pl.multiple_of(512 * which, 512), 512)
        return jnp.dot(act[k, :, units], w_down[k, units, :], preferred_element_type=F32)

    def mlp_out(k, target, arrival):
        u_buf[...] = mlp_half(k, core)
        if arrival is not None:
            arrival.wait()
        value = u_buf[...] + mlp_half(k, 1 - core) + w32[k, 59:60, :]
        branch[k] = value
        result = wide_mask() * (dense[...] + w32[k, 60:61, :] * value)
        target[...] = result.astype(BF16).astype(F32)

    def put_small(row, total):
        small[7, row : row + 1, :] = total[:, 0:128]
        small[7, row + 5 : row + 6, :] = total[:, 128:256]

    def mlp_back(k):
        e = wide_mask() * cot[...]
        e_buf[...] = e
        put_small(4, jnp.sum(e * branch[k], axis=0, keepdims=True))
        dm_wide = (w32[k, 60:61, :] * e).astype(BF16)
        dm_buf[...] = dm_wide
        put_small(3, jnp.sum(dm_wide.astype(F32), axis=0, keepdims=True))
        u_buf[...] = jnp.zeros((CELLS, C), F32)

        def chunk(step, carry):
            i = (step + 2 * (1 - core)) % 4
            cols = pl.ds(pl.multiple_of(256 * i, 256), 256)
            dm = dm_buf[...]
            da = lax.dot_general(dm, w_down[k, cols, :], cols_contract, preferred_element_type=F32)
            dh = (da * slope[k, :, cols]).astype(BF16)
            bias = jnp.sum(dh.astype(F32), axis=0, keepdims=True)
            u_buf[...] += lax.dot_general(dh, w_up[k, :, cols], cols_contract, preferred_element_type=F32)
            gup = lax.dot_general(z_buf[k], dh, rows_contract, preferred_element_type=F32).astype(BF16)
            gdown = lax.dot_general(act[k, :, cols], dm, rows_contract, preferred_element_type=F32).astype(BF16)
            for t in range(2):
                slab = 2 * i + t
                cut = slice(128 * t, 128 * (t + 1))
                small[slab, 14:15, :] = bias[:, cut]
                slabs[k, slab, 0:256, :] = gup[:, cut]
                slabs[k, slab, 256:384, :] = gdown[cut, 0:128]
                slabs[k, slab, 384:512, :] = gdown[cut, 128:256]
            return carry

        lax.fori_loop(0, 2, chunk, 0)
        core_big(k)
        lax.fori_loop(2, 4, chunk, 0)
        dz = u_buf[...]
        put_small(1, jnp.sum(dz * normed[k], axis=0, keepdims=True))
        put_small(2, jnp.sum(dz, axis=0, keepdims=True))
        dn = dz * w32[k, 57:58, :]
        first = jnp.mean(dn, axis=-1, keepdims=True)
        second = jnp.mean(dn * normed[k], axis=-1, keepdims=True)
        du = (inv[k] * (dn - first - normed[k] * second)).astype(BF16).astype(F32)
        du_buf[...] = du
        put_small(0, jnp.sum(du, axis=0, keepdims=True))

    other = pl.ds(4 * (1 - core), 4)
    mine4 = 4 * core
    my_slab = mine4 + first

    def sem(k, number):
        return S_SUM + N_SUM * k + number

    def core_copy(k, i):
        return remote(
            slabs.at[k, 4 * (1 - core) + i, pl.ds(0, BIG)], r_core.at[k, i, pl.ds(0, BIG)], sem(k, L_CORE + i), sibling
        )

    def core_big(k):
        for i in range(4):
            core_copy(k, i).start()

    def core_small_copy(k):
        return remote(
            slabs.at[k, other, pl.ds(BIG, 16)], r_core.at[k, :, pl.ds(BIG, 16)], sem(k, L_CORES), sibling
        )

    def core_small(k):
        for slab in range(8):
            slabs[k, slab, BIG:SLAB, :] = small[slab].astype(BF16)
        core_small_copy(k).start()

    def first_add(k, i, rows):
        total = slabs[k, mine4 + i, rows, :].astype(F32) + r_core[k, i, rows, :].astype(F32)
        half[k, i, rows, :] = total.astype(BF16)

    def first_copy(k, d, low, size, number):
        span = pl.ds(low, size)
        return remote(
            half.at[k, (first + d) % 4, span], r_f.at[k, d - 1, span], sem(k, number + d - 1), first_peer(d)
        )

    def first_big(k):
        for i in range(4):
            core_copy(k, i).wait()
        for d in range(1, 4):
            first_add(k, (first + d) % 4, slice(0, BIG))
            first_copy(k, d, 0, BIG, L_F).start()
        first_add(k, first, slice(0, BIG))

    def first_small(k):
        core_small_copy(k).wait()
        for i in range(4):
            first_add(k, i, slice(BIG, SLAB))
        for d in range(1, 4):
            first_copy(k, d, BIG, 16, L_FS).start()

    def second_copy(k, d):
        return remote(t_all.at[k, (second + d) % 4], r_g.at[k, second], sem(k, L_G + d - 1), second_peer(d))

    def second_phase(k):
        for d in range(1, 4):
            first_copy(k, d, 0, BIG, L_F).wait()
            first_copy(k, d, BIG, 16, L_FS).wait()

        def total(rows):
            value = half[k, first, rows, :].astype(F32)
            for d in range(3):
                value = value + r_f[k, d, rows, :].astype(F32)
            return value.astype(BF16)

        tail = total(slice(BIG, SLAB))
        for i in range(4):
            t_all[k, i, 0:128, :] = total(slice(128 * i, 128 * (i + 1)))
            t_all[k, i, 128:144, :] = tail
        for d in range(1, 4):
            second_copy(k, d).start()
        r_g[k, second] = t_all[k, second]

    def z_copy(k, d):
        return remote(u_all.at[k, (z + d) % N_Z], r_z.at[k, z], sem(k, L_Z + d - 1), z_peer(d))

    def z_phase(k):
        for d in range(1, 4):
            second_copy(k, d).wait()
        value = r_g[k, 0].astype(F32)
        for i in range(1, 4):
            value = value + r_g[k, i].astype(F32)
        value = value.astype(BF16)
        for i in range(N_Z):
            u_all[k, i, 0:16, :] = value[16 * i : 16 * (i + 1)]
            u_all[k, i, 16:32, :] = value[128:144]
        for d in range(1, N_Z):
            z_copy(k, d).start()
        r_z[k, z] = u_all[k, z]

    my_rows = pl.ds(pl.multiple_of(16 * z, 16), 16)
    plane = [(dx, dy) for dx in range(4) for dy in range(4) if dx or dy]

    def back_z_copy(k, d):
        spot = full.at[k, my_slab, second, my_rows]
        return remote(spot, spot, sem(k, L_AZ + d - 1), z_peer(d))

    def plane_copy(k, dx, dy):
        spot = full.at[k, my_slab, second]
        return remote(spot, spot, sem(k, L_AP + 4 * dx + dy - 1), placed((ring + dx) % 4, (y + dy) % N_Y))

    def back_core_copy(k, dx, dy):
        xx, yy = (ring + 4 - dx) % 4, (y + N_Y - dy) % N_Y
        spot = full.at[k, mine4 + yy * (1 - core) + xx * core, xx * (1 - core) + yy * core]
        return remote(spot, spot, sem(k, L_AC + 4 * dx + dy), sibling)

    def reached(k, dx):
        return (ring + dx) % 4 // 2 == k

    def back_z(k):
        for d in range(1, N_Z):
            z_copy(k, d).wait()
        value = r_z[k, 0].astype(F32)
        for i in range(1, N_Z):
            value = value + r_z[k, i].astype(F32)
        value = value.astype(BF16)
        full[k, my_slab, second, my_rows, :] = value[0:16]
        full[k, my_slab, second, 128:144, :] = value[16:32]
        for d in range(1, N_Z):
            back_z_copy(k, d).start()

    def back_plane(k):
        for d in range(1, N_Z):
            back_z_copy(k, d).wait()
        for dx in range(4):

            @pl.when(reached(k, dx))
            def _(dx=dx):
                for dy in range(N_Y):
                    if dx or dy:
                        plane_copy(k, dx, dy).start()

    def back_core(k):
        @pl.when(sec == k)
        def _():
            back_core_copy(k, 0, 0).start()
            for dx, dy in plane:
                plane_copy(k, dx, dy).wait_recv()
                back_core_copy(k, dx, dy).start()
            pltpu.make_async_copy(
                full.at[k, pl.ds(mine4, 4)], sums_ref.at[pl.ds(mine4, 4)], local.at[D_FULL]
            ).start()

        for dx in range(4):

            @pl.when(reached(k, dx))
            def _(dx=dx):
                for dy in range(N_Y):
                    if dx or dy:
                        plane_copy(k, dx, dy).wait_send()

    def back_end(k):
        @pl.when(sec == k)
        def _():
            for dx in range(4):
                for dy in range(N_Y):
                    back_core_copy(k, dx, dy).wait()
            rest = pltpu.make_async_copy(full.at[k, other], sums_ref.at[other], local.at[D_FULL + 1])
            rest.start()
            pltpu.make_async_copy(
                full.at[k, pl.ds(mine4, 4)], sums_ref.at[pl.ds(mine4, 4)], local.at[D_FULL]
            ).wait()
            rest.wait()

    def own_out(k):
        return pltpu.make_async_copy(o_send.at[k, lat], out_ref.at[k, pl.ds(COLS * lat, COLS)], local.at[D_OUT + k])

    def out_copy(k, d, peer, sample, number):
        return remote(
            o_send.at[k, (lat + d) % 4], out_ref.at[sample, pl.ds(COLS * lat, COLS)], number + d, peer
        )

    def out_start(k, field):
        g3[...] = field[...].reshape(COLS, ROWS, C)
        for a in range(N_LAT):
            o_send[k, a] = g3[:, 4 * a : 4 * a + 4, :].astype(BF16)

        @pl.when(sec == k)
        def _():
            own_out(k).start()
            for d in range(1, 4):
                out_copy(k, d, lat_peer(d), k, S_OWN).start()

        @pl.when(sec != k)
        def _():
            for d in range(4):
                out_copy(k, d, cross_peer(d), 1 - k, S_CROSS).start()

    def out_end(k):
        @pl.when(sec == k)
        def _():
            own_out(k).wait()
            for d in range(1, 4):
                out_copy(k, d, lat_peer(d), k, S_OWN).wait()
            for d in range(4):
                out_copy(k, d, cross_peer(d), 1 - k, S_CROSS).wait_recv()

        @pl.when(sec != k)
        def _():
            for d in range(4):
                out_copy(k, d, cross_peer(d), 1 - k, S_CROSS).wait_send()

    a_x[lat] = x_own[pl.ds(COLS * lat, COLS)]
    for copy in x_in:
        copy.wait()
    gather(a_x, dense)
    copies = halo_start(dense, 0)
    for copy in m_in:
        copy.wait()
    gather_mask()
    sm_in.wait()
    for k in range(2):
        w32[k] = w_sm[k].astype(F32)
    inner_columns(dense, 0, 0, False, u_buf)
    outer_columns(copies, 0, 0, 0, False, u_buf)
    normalise(0)
    up_in.wait()
    their_up = w_up.at[1 - sec, :, up_cols]
    up_fwd = push(their_up, their_up, S_UPF, sibling)
    own_up.wait()
    mlp_hidden(0, 0, 2)
    up_fwd.wait()
    mlp_hidden(0, 2, 4)
    down_in.wait()
    their_down = w_down.at[1 - sec, down_rows]
    down_fwd = push(their_down, their_down, S_DOWNF, sibling)
    own_down.wait()
    mlp_out(0, cot, down_fwd)
    dense[...] = cot[...]
    copies = halo_start(dense, 1)
    c_in = [push(strip(c_ref, (lat + d) % 4), a_c.at[lat], S_C + d - 1, lat_peer(d)) for d in range(1, 4)]
    own_c.start()
    inner_columns(dense, 1, 1, False, u_buf)
    outer_columns(copies, 1, 1, 1, False, u_buf)
    normalise(1)
    mlp_hidden(1, 0, 4)
    mlp_out(1, cot, None)
    out_start(1, cot)

    own_c.wait()
    for copy in c_in:
        copy.wait()
    gather(a_c, cot)
    mlp_back(1)
    copies = halo_start(du_buf, 2)
    first_big(1)
    tap_grads(1)
    core_small(1)
    inner_columns(du_buf, 2, 1, True, u_buf)
    outer_columns(copies, 2, 2, 1, True, u_buf)
    cot[...] = (e_buf[...] + u_buf[...]).astype(BF16).astype(F32)
    first_small(1)

    mlp_back(0)
    copies = halo_start(du_buf, 3)
    first_big(0)
    tap_grads(0)
    core_small(0)
    second_phase(1)
    first_small(0)
    z_phase(1)
    inner_columns(du_buf, 2, 0, True, u_buf)
    second_phase(0)
    outer_columns(copies, 3, 2, 0, True, u_buf)
    z_phase(0)
    cot[...] = (e_buf[...] + u_buf[...]).astype(BF16).astype(F32)
    out_start(0, cot)
    back_z(1)
    back_z(0)
    back_plane(1)
    back_plane(0)
    back_core(1)
    back_core(0)
    out_end(1)
    out_end(0)
    back_end(1)
    back_end(0)


def unpack_kernel(
    sums, raw, out_ref, gup_ref, gdown_ref, taps_ref, chans_ref, bias_ref, held, raw_held, wide, tall, done
):
    loads = [pltpu.make_async_copy(sums.at[i], held.at[i], done.at[i]) for i in range(8)]
    raw_in = pltpu.make_async_copy(raw, raw_held, done.at[24])
    raw_out = pltpu.make_async_copy(raw_held, out_ref, done.at[25])
    for load in loads[:2]:
        load.start()
    raw_in.start()
    for load in loads[2:]:
        load.start()
    stores = []
    for i in range(8):
        loads[i].wait()
        cols = pl.ds(128 * i, 128)
        for g in range(2):
            part = slice(128 * g, 128 * (g + 1))
            wide[i, part, :] = held[i, g, 0:128, :].astype(F32) * factor
            tall[i, :, part] = held[i, 2 + g, 0:128, :].astype(F32) * factor
        stores.append(pltpu.make_async_copy(wide.at[i], gup_ref.at[:, cols], done.at[8 + i]))
        stores.append(pltpu.make_async_copy(tall.at[i], gdown_ref.at[cols], done.at[16 + i]))
        stores[-2].start()
        stores[-1].start()
        if i == 2:
            raw_in.wait()
            raw_out.start()
        piece = held[i, 0, 128:144, :].astype(F32) * factor
        bias_ref[:, 128 * i : 128 * (i + 1)] = piece[14:15]
        for h in range(2):
            lanes = slice(128 * h, 128 * (h + 1))
            if i < 7:
                for q in range(7):
                    taps_ref[7 * i + q, :, lanes] = piece[7 * h + q : 7 * h + q + 1]
            else:
                for r in range(5):
                    chans_ref[r, :, lanes] = piece[5 * h + r : 5 * h + r + 1]
    raw_out.wait()
    for store in stores:
        store.wait()


def on_device(
    window_input,
    output_cotangent,
    ocean_mask,
    dw_kernel,
    channel_params,
    up_weight,
    up_bias,
    down_weight,
):
    vmem = pl.BlockSpec(memory_space=pltpu.VMEM)
    hbm = pl.BlockSpec(memory_space=pl.ANY)
    raw, sums = pl.pallas_call(
        step_kernel,
        out_shape=(
            jax.ShapeDtypeStruct((2, PART, 4, C), BF16),
            jax.ShapeDtypeStruct((8, 4, 144, 128), BF16),
        ),
        in_specs=[hbm, hbm, vmem, vmem, vmem, vmem, hbm, hbm],
        out_specs=(hbm, hbm),
        scratch_shapes=[
            pltpu.VMEM((2, 256, 1024), BF16),
            pltpu.VMEM((2, 1024, 256), BF16),
            pltpu.VMEM((2, 80, C), BF16),
            pltpu.VMEM((2, 80, C), F32),
            pltpu.VMEM((80, C), F32),
            pltpu.VMEM((8, 128), F32),
            pltpu.VMEM((PART, 4, C), BF16),
            pltpu.VMEM((4, COLS, 4, C), BF16),
            pltpu.VMEM((4, COLS, 4, C), BF16),
            pltpu.VMEM((4, 8, 128), F32),
            pltpu.VMEM((COLS, ROWS, C), F32),
            pltpu.VMEM((CELLS, C), F32),
            pltpu.VMEM((CELLS, 128), F32),
            pltpu.VMEM((COLS + 6, 32, C), F32),
            pltpu.VMEM((3, 7, COLS + 6, ROWS, C), F32),
            pltpu.VMEM((4, 2, EDGE, C), BF16),
            pltpu.VMEM((4, 2, EDGE, C), BF16),
            pltpu.VMEM((CELLS, C), F32),
            pltpu.VMEM((2, CELLS, C), F32),
            pltpu.VMEM((2, CELLS, 1), F32),
            pltpu.VMEM((2, CELLS, C), BF16),
            pltpu.VMEM((2, CELLS, 1024), BF16),
            pltpu.VMEM((2, CELLS, 1024), F32),
            pltpu.VMEM((2, CELLS, C), F32),
            pltpu.VMEM((CELLS, C), F32),
            pltpu.VMEM((CELLS, C), BF16),
            pltpu.VMEM((CELLS, C), F32),
            pltpu.VMEM((CELLS, C), F32),
            pltpu.VMEM((2, 8, SLAB, 128), BF16),
            pltpu.VMEM((8, 16, 128), F32),
            pltpu.VMEM((2, 4, SLAB, 128), BF16),
            pltpu.VMEM((2, 4, SLAB, 128), BF16),
            pltpu.VMEM((2, 3, SLAB, 128), BF16),
            pltpu.VMEM((2, 4, 144, 128), BF16),
            pltpu.VMEM((2, 4, 144, 128), BF16),
            pltpu.VMEM((2, 8, 32, 128), BF16),
            pltpu.VMEM((2, 8, 32, 128), BF16),
            pltpu.VMEM((2, 8, 4, 144, 128), BF16),
            pltpu.VMEM((2, 4, COLS, 4, C), BF16),
            pltpu.SemaphoreType.DMA((N_LOCAL,)),
            pltpu.SemaphoreType.DMA((N_SEM,)),
            pltpu.SemaphoreType.DMA((N_SEM,)),
        ],
        compiler_params=pltpu.CompilerParams(
            collective_id=0, has_side_effects=True, vmem_limit_bytes=56 << 20
        ),
        name="two_blocks",
    )(
        window_input.transpose(0, 2, 1, 3),
        output_cotangent.transpose(0, 2, 1, 3),
        ocean_mask,
        dw_kernel[0],
        channel_params[0],
        up_bias,
        up_weight[0],
        down_weight[0],
    )
    boundary, gup, gdown, taps, chans, gbias = pl.pallas_call(
        unpack_kernel,
        out_shape=(
            jax.ShapeDtypeStruct((2, PART, 4, C), BF16),
            jax.ShapeDtypeStruct((256, 1024), F32),
            jax.ShapeDtypeStruct((1024, 256), F32),
            jax.ShapeDtypeStruct((49, 1, C), F32),
            jax.ShapeDtypeStruct((5, 1, C), F32),
            jax.ShapeDtypeStruct((1, 1024), F32),
        ),
        in_specs=[hbm, hbm],
        out_specs=(hbm, hbm, hbm, vmem, vmem, vmem),
        scratch_shapes=[
            pltpu.VMEM((8, 4, 144, 128), BF16),
            pltpu.VMEM((2, PART, 4, C), BF16),
            pltpu.VMEM((8, 256, 128), F32),
            pltpu.VMEM((8, 128, 256), F32),
            pltpu.SemaphoreType.DMA((26,)),
        ],
        compiler_params=pltpu.CompilerParams(vmem_limit_bytes=60 << 20),
        name="unpack",
    )(sums, raw)
    return (
        boundary.transpose(0, 2, 1, 3)[None],
        taps.transpose(1, 0, 2),
        chans.transpose(1, 0, 2),
        gup[None],
        gbias,
        gdown[None],
    )


def solution(mesh):
    in_specs = (
        P(None, "lat", "lon", None),
        P(None, "lat", "lon", None),
        P("lat", "lon"),
        P("section", None, None),
        P("section", None, None),
        P("section", None, None),
        P("section", None),
        P("section", None, None),
    )
    out_specs = (
        P("section", None, "lat", "lon", None),
        P("section", None, None),
        P("section", None, None),
        P("section", None, None),
        P("section", None),
        P("section", None, None),
    )
    return jax.shard_map(
        on_device, mesh=mesh, in_specs=in_specs, out_specs=out_specs, check_vma=False
    )
```

```python
import functools
import math

import jax
import jax.numpy as jnp
from jax import lax
from jax.experimental import pallas as pl
from jax.experimental.pallas import tpu as pltpu
from jax.sharding import PartitionSpec as P

MESH = pl.DeviceIdType.MESH
F32 = jnp.float32
BF16 = jnp.bfloat16
N_LAT = 4
N_LON = 32
N_Y = 4
N_Z = 8
COLS = 17
ROWS = 16
CELLS = COLS * ROWS
PART = 68
EDGE = 3 * ROWS
C = 256
BIG = 512
SLAB = 528

norm_eps = 1e-06
gelu_scale = 0.7978845608028654
gelu_cubic = 0.044715
factor = 1.0 / math.sqrt(544)
rows_contract = (((0,), (0,)), ((), ()))
cols_contract = (((1,), (1,)), ((), ()))

S_SMALL, S_UP, S_DOWN, S_UPF, S_DOWNF = 0, 1, 2, 3, 4
S_X, S_M, S_C = 5, 8, 11
S_HALO = 14
S_OWN, S_CROSS = 22, 26
S_SUM = 30
L_CORE, L_CORES, L_F, L_FS, L_G, L_Z = 0, 4, 5, 8, 11, 14
L_AZ, L_AP, L_AC = 21, 28, 43
N_SUM = 59
N_SEM = S_SUM + 2 * N_SUM
D_UP, D_DOWN, D_X, D_C, D_OUT, D_FULL = 0, 1, 2, 3, 4, 6
N_LOCAL = 10


def step_kernel(
    x_ref, c_ref, m_ref, taps_ref, par_ref, bias_ref, up_ref, down_ref,
    out_ref, sums_ref,
    w_up, w_down, w_sm, w32, sw, m_own,
    x_own, a_x, a_c, a_m, g3,
    dense, mask, pad, shifted, edge_out, edge_in,
    u_buf, normed, inv, z_buf, act, slope, branch, e_buf, dm_buf, du_buf, cot,
    slabs, small, r_core, half, r_f, t_all, r_g, u_all, r_z, full,
    o_send,
    local, send, recv,
):
    sec = lax.axis_index("section")
    lat = lax.axis_index("lat")
    lon = lax.axis_index("lon")
    x, core = lat // 2, lat % 2
    y, z = lon // N_Z, lon % N_Z
    ring = 2 * sec + x

    sibling = {"lat": x * 2 + (1 - core)}
    partner = {"section": 1 - sec, "lat": (1 - x) * 2 + core}
    right = {"lat": (lat + 1) % N_LAT, "lon": (lon + (lat + 1) // N_LAT) % N_LON}
    left = {"lat": (lat + 3) % N_LAT, "lon": (lon + N_LON - 1 + (lat + 3) // N_LAT) % N_LON}

    def lat_peer(d):
        return {"lat": (lat + d) % N_LAT}

    def cross_peer(d):
        return {"section": 1 - sec, "lat": (lat + d) % N_LAT}

    def y_peer(d):
        return {"lon": (y + d) % N_Y * N_Z + z}

    def z_peer(d):
        return {"lon": y * N_Z + (z + d) % N_Z}

    def remote(source, target, slot, peer):
        return pltpu.make_async_remote_copy(
            src_ref=source,
            dst_ref=target,
            send_sem=send.at[slot],
            recv_sem=recv.at[slot],
            device_id=peer,
            device_id_type=MESH,
        )

    def push(source, target, slot, peer):
        copy = remote(source, target, slot, peer)
        copy.start()
        return copy

    def placed(xx, yy):
        return {"section": xx // 2, "lat": xx % 2 * 2 + core, "lon": yy * N_Z + z}

    first = y * (1 - core) + ring * core
    second = ring * (1 - core) + y * core

    def first_peer(d):
        return placed((ring + d * core) % 4, (y + d * (1 - core)) % N_Y)

    def second_peer(d):
        return placed((ring + d * (1 - core)) % 4, (y + d * core) % N_Y)

    peers = [lat_peer(d) for d in range(1, 4)] + [cross_peer(d) for d in range(4)] + [left, right]
    peers += [placed((ring + dx) % 4, (y + dy) % N_Y) for dx in range(4) for dy in range(1, N_Y)]
    peers += [z_peer(d) for d in range(1, N_Z)]
    barrier = pltpu.get_barrier_semaphore()
    for peer in peers:
        pl.semaphore_signal(barrier, inc=1, device_id=peer, device_id_type=MESH)

    fetch = pltpu.make_async_copy(x_ref.at[sec], x_own, local.at[D_X])
    fetch.start()
    sw[...] = jnp.zeros_like(sw)
    for p in range(7):
        sw[8 * p : 8 * p + 7, :] = taps_ref[7 * p : 7 * p + 7, :].astype(F32)
    sw[56:61, :] = par_ref[...].astype(F32)
    for i in range(4):
        sw[64 + i : 65 + i, :] = bias_ref[:, 256 * i : 256 * (i + 1)].astype(F32)
    w_sm[sec] = sw[...].astype(BF16)
    m_own[...] = jnp.zeros_like(m_own)
    m_own[0:4, 0:PART] = m_ref[...].astype(F32)

    pl.semaphore_wait(barrier, len(peers))

    def strip(ref, b):
        return ref.at[sec, pl.ds(COLS * b, COLS)]

    def x_strip(b):
        return x_own.at[pl.ds(COLS * b, COLS)]

    fetch.wait()
    x_in = [push(x_strip((lat + d) % 4), a_x.at[lat], S_X + d - 1, lat_peer(d)) for d in range(1, 4)]
    m_in = [push(m_own, a_m.at[lat], S_M + d - 1, lat_peer(d)) for d in range(1, 4)]
    sm_in = push(w_sm.at[sec], w_sm.at[sec], S_SMALL, partner)
    own_up = pltpu.make_async_copy(up_ref, w_up.at[sec], local.at[D_UP])
    own_down = pltpu.make_async_copy(down_ref, w_down.at[sec], local.at[D_DOWN])
    own_c = pltpu.make_async_copy(strip(c_ref, lat), a_c.at[lat], local.at[D_C])
    own_up.start()
    own_down.start()
    up_cols = pl.ds(pl.multiple_of(core * 512, 512), 512)
    down_rows = pl.ds(pl.multiple_of(core * 512, 512), 512)
    up_in = push(up_ref.at[:, up_cols], w_up.at[sec, :, up_cols], S_UP, partner)
    down_in = push(down_ref.at[down_rows], w_down.at[sec, down_rows], S_DOWN, partner)

    a_m[lat] = m_own[...]
    pad[:, 0:8, :] = jnp.zeros((COLS + 6, 8, C), F32)
    pad[:, 24:32, :] = jnp.zeros((COLS + 6, 8, C), F32)
    small[...] = jnp.zeros_like(small)

    def gather(parts, target):
        for a in range(N_LAT):
            g3[:, 4 * a : 4 * a + 4, :] = parts[a].astype(F32)
        target[...] = g3[...].reshape(CELLS, C)

    def gather_mask():
        rows = jnp.concatenate([a_m[a, 0:4, :] for a in range(N_LAT)], axis=0)
        shape = (COLS, ROWS, 128)
        wanted = COLS * lat + lax.broadcasted_iota(jnp.int32, shape, 0)
        picked = jnp.where(lax.broadcasted_iota(jnp.int32, shape, 2) == wanted, rows[None], 0.0)
        value = jnp.sum(picked, axis=-1, keepdims=True)
        mask[...] = jnp.broadcast_to(value, shape).reshape(CELLS, 128)

    def halo_start(field, number):
        edge_out[number, 0] = field[CELLS - EDGE : CELLS, :].astype(BF16)
        edge_out[number, 1] = field[0:EDGE, :].astype(BF16)
        base = S_HALO + 2 * number
        return [
            push(edge_out.at[number, 0], edge_in.at[number, 0], base, right),
            push(edge_out.at[number, 1], edge_in.at[number, 1], base + 1, left),
        ]

    def shift_columns(slot, low, high):
        def shift(col, carry):
            for p in range(7):
                shifted[slot, p, col] = pad[col, 5 + p : 21 + p, :]
            return carry

        lax.fori_loop(low, high, shift, 0)

    def stencil(slot, k, reverse, target, low, count):
        for h in range(2):
            lanes = slice(128 * h, 128 * (h + 1))

            def tap_row(p, acc):
                taps = w32[k, pl.ds(pl.multiple_of(8 * ((6 - p) if reverse else p), 8), 8), lanes]
                for q in range(7):
                    row = 6 - q if reverse else q
                    window = shifted[slot, p, low + q : low + q + count, :, lanes]
                    acc = acc + window * taps[row : row + 1, :][None]
                return acc

            acc = lax.fori_loop(0, 7, tap_row, jnp.zeros((count, ROWS, 128), F32))
            target[ROWS * low : ROWS * (low + count), lanes] = acc.reshape(ROWS * count, 128)

    def inner_columns(field, slot, k, reverse, target):
        for j in range(COLS):
            pad[3 + j, 8:24, :] = field[ROWS * j : ROWS * (j + 1), :]
        shift_columns(slot, 3, COLS + 3)
        stencil(slot, k, reverse, target, 3, COLS - 6)

    def outer_columns(copies, number, slot, k, reverse, target):
        for copy in copies:
            copy.wait()
        for j in range(3):
            rows = slice(ROWS * j, ROWS * (j + 1))
            pad[j, 8:24, :] = edge_in[number, 0, rows, :].astype(F32)
            pad[COLS + 3 + j, 8:24, :] = edge_in[number, 1, rows, :].astype(F32)
        shift_columns(slot, 0, 3)
        shift_columns(slot, COLS + 3, COLS + 6)
        stencil(slot, k, reverse, target, 0, 3)
        stencil(slot, k, reverse, target, COLS - 3, 3)

    def tap_grads(k):
        for h in range(2):
            lanes = slice(128 * h, 128 * (h + 1))

            def tap_row(p, carry):
                grad = du_buf[:, lanes].reshape(COLS, ROWS, 128)
                for q in range(7):
                    window = shifted[k, p, q : q + COLS, :, lanes]
                    total = jnp.sum((grad * window).reshape(CELLS, 128), axis=0, keepdims=True)
                    small[p, 7 * h + q : 7 * h + q + 1, :] = total
                return carry

            lax.fori_loop(0, 7, tap_row, 0)

    def wide_mask():
        return jnp.concatenate([mask[...], mask[...]], axis=1)

    def normalise(k):
        u = u_buf[...] + w32[k, 56:57, :]
        centered = u - jnp.mean(u, axis=-1, keepdims=True)
        inverse = lax.rsqrt(jnp.mean(centered * centered, axis=-1, keepdims=True) + norm_eps)
        value = centered * inverse
        inv[k] = inverse
        normed[k] = value
        z_buf[k] = (value * w32[k, 57:58, :] + w32[k, 58:59, :]).astype(BF16)

    def mlp_hidden(k, low, high):
        def chunk(step, carry):
            i = (step + 2 * core) % 4
            cols = pl.ds(pl.multiple_of(256 * i, 256), 256)
            hidden = jnp.dot(z_buf[k], w_up[k, :, cols], preferred_element_type=F32)
            hidden = hidden + w32[k, pl.ds(64 + i, 1), :]
            square = hidden * hidden
            tangent = jnp.tanh(gelu_scale * (hidden + gelu_cubic * square * hidden))
            act[k, :, cols] = (0.5 * hidden * (1.0 + tangent)).astype(BF16)
            slope[k, :, cols] = 0.5 * (1.0 + tangent) + 0.5 * hidden * (1.0 - tangent * tangent) * gelu_scale * (
                1.0 + 3.0 * gelu_cubic * square
            )
            return carry

        lax.fori_loop(low, high, chunk, 0)

    def mlp_half(k, which):
        units = pl.ds(pl.multiple_of(512 * which, 512), 512)
        return jnp.dot(act[k, :, units], w_down[k, units, :], preferred_element_type=F32)

    def mlp_out(k, target, arrival):
        u_buf[...] = mlp_half(k, core)
        if arrival is not None:
            arrival.wait()
        value = u_buf[...] + mlp_half(k, 1 - core) + w32[k, 59:60, :]
        branch[k] = value
        result = wide_mask() * (dense[...] + w32[k, 60:61, :] * value)
        target[...] = result.astype(BF16).astype(F32)

    def put_small(row, total):
        small[7, row : row + 1, :] = total[:, 0:128]
        small[7, row + 5 : row + 6, :] = total[:, 128:256]

    def mlp_back(k):
        e = wide_mask() * cot[...]
        e_buf[...] = e
        put_small(4, jnp.sum(e * branch[k], axis=0, keepdims=True))
        dm_wide = (w32[k, 60:61, :] * e).astype(BF16)
        dm_buf[...] = dm_wide
        put_small(3, jnp.sum(dm_wide.astype(F32), axis=0, keepdims=True))
        u_buf[...] = jnp.zeros((CELLS, C), F32)

        def chunk(step, carry):
            i = (step + 2 * (1 - core)) % 4
            cols = pl.ds(pl.multiple_of(256 * i, 256), 256)
            dm = dm_buf[...]
            da = lax.dot_general(dm, w_down[k, cols, :], cols_contract, preferred_element_type=F32)
            dh = (da * slope[k, :, cols]).astype(BF16)
            bias = jnp.sum(dh.astype(F32), axis=0, keepdims=True)
            u_buf[...] += lax.dot_general(dh, w_up[k, :, cols], cols_contract, preferred_element_type=F32)
            gup = lax.dot_general(z_buf[k], dh, rows_contract, preferred_element_type=F32).astype(BF16)
            gdown = lax.dot_general(act[k, :, cols], dm, rows_contract, preferred_element_type=F32).astype(BF16)
            for t in range(2):
                slab = 2 * i + t
                cut = slice(128 * t, 128 * (t + 1))
                small[slab, 14:15, :] = bias[:, cut]
                slabs[k, slab, 0:256, :] = gup[:, cut]
                slabs[k, slab, 256:384, :] = gdown[cut, 0:128]
                slabs[k, slab, 384:512, :] = gdown[cut, 128:256]
            return carry

        lax.fori_loop(0, 2, chunk, 0)
        core_big(k)
        lax.fori_loop(2, 4, chunk, 0)
        dz = u_buf[...]
        put_small(1, jnp.sum(dz * normed[k], axis=0, keepdims=True))
        put_small(2, jnp.sum(dz, axis=0, keepdims=True))
        dn = dz * w32[k, 57:58, :]
        first = jnp.mean(dn, axis=-1, keepdims=True)
        second = jnp.mean(dn * normed[k], axis=-1, keepdims=True)
        du = (inv[k] * (dn - first - normed[k] * second)).astype(BF16).astype(F32)
        du_buf[...] = du
        put_small(0, jnp.sum(du, axis=0, keepdims=True))

    other = pl.ds(4 * (1 - core), 4)
    mine4 = 4 * core
    my_slab = mine4 + first

    def sem(k, number):
        return S_SUM + N_SUM * k + number

    def core_copy(k, i):
        return remote(
            slabs.at[k, 4 * (1 - core) + i, pl.ds(0, BIG)], r_core.at[k, i, pl.ds(0, BIG)], sem(k, L_CORE + i), sibling
        )

    def core_big(k):
        for i in range(4):
            core_copy(k, i).start()

    def core_small_copy(k):
        return remote(
            slabs.at[k, other, pl.ds(BIG, 16)], r_core.at[k, :, pl.ds(BIG, 16)], sem(k, L_CORES), sibling
        )

    def core_small(k):
        for slab in range(8):
            slabs[k, slab, BIG:SLAB, :] = small[slab].astype(BF16)
        core_small_copy(k).start()

    def first_add(k, i, rows):
        total = slabs[k, mine4 + i, rows, :].astype(F32) + r_core[k, i, rows, :].astype(F32)
        half[k, i, rows, :] = total.astype(BF16)

    def first_copy(k, d, low, size, number):
        span = pl.ds(low, size)
        return remote(
            half.at[k, (first + d) % 4, span], r_f.at[k, d - 1, span], sem(k, number + d - 1), first_peer(d)
        )

    def first_big(k):
        for i in range(4):
            core_copy(k, i).wait()
        for d in range(1, 4):
            first_add(k, (first + d) % 4, slice(0, BIG))
            first_copy(k, d, 0, BIG, L_F).start()
        first_add(k, first, slice(0, BIG))

    def first_small(k):
        core_small_copy(k).wait()
        for i in range(4):
            first_add(k, i, slice(BIG, SLAB))
        for d in range(1, 4):
            first_copy(k, d, BIG, 16, L_FS).start()

    def second_copy(k, d):
        return remote(t_all.at[k, (second + d) % 4], r_g.at[k, second], sem(k, L_G + d - 1), second_peer(d))

    def second_phase(k):
        for d in range(1, 4):
            first_copy(k, d, 0, BIG, L_F).wait()
            first_copy(k, d, BIG, 16, L_FS).wait()

        def total(rows):
            value = half[k, first, rows, :].astype(F32)
            for d in range(3):
                value = value + r_f[k, d, rows, :].astype(F32)
            return value.astype(BF16)

        tail = total(slice(BIG, SLAB))
        for i in range(4):
            t_all[k, i, 0:128, :] = total(slice(128 * i, 128 * (i + 1)))
            t_all[k, i, 128:144, :] = tail
        for d in range(1, 4):
            second_copy(k, d).start()
        r_g[k, second] = t_all[k, second]

    def z_copy(k, d):
        return remote(u_all.at[k, (z + d) % N_Z], r_z.at[k, z], sem(k, L_Z + d - 1), z_peer(d))

    def z_phase(k):
        for d in range(1, 4):
            second_copy(k, d).wait()
        value = r_g[k, 0].astype(F32)
        for i in range(1, 4):
            value = value + r_g[k, i].astype(F32)
        value = value.astype(BF16)
        for i in range(N_Z):
            u_all[k, i, 0:16, :] = value[16 * i : 16 * (i + 1)]
            u_all[k, i, 16:32, :] = value[128:144]
        for d in range(1, N_Z):
            z_copy(k, d).start()
        r_z[k, z] = u_all[k, z]

    my_rows = pl.ds(pl.multiple_of(16 * z, 16), 16)
    plane = [(dx, dy) for dx in range(4) for dy in range(4) if dx or dy]

    def back_z_copy(k, d):
        spot = full.at[k, my_slab, second, my_rows]
        return remote(spot, spot, sem(k, L_AZ + d - 1), z_peer(d))

    def plane_copy(k, dx, dy):
        spot = full.at[k, my_slab, second]
        return remote(spot, spot, sem(k, L_AP + 4 * dx + dy - 1), placed((ring + dx) % 4, (y + dy) % N_Y))

    def back_core_copy(k, dx, dy):
        xx, yy = (ring + 4 - dx) % 4, (y + N_Y - dy) % N_Y
        spot = full.at[k, mine4 + yy * (1 - core) + xx * core, xx * (1 - core) + yy * core]
        return remote(spot, spot, sem(k, L_AC + 4 * dx + dy), sibling)

    def reached(k, dx):
        return (ring + dx) % 4 // 2 == k

    def back_z(k):
        for d in range(1, N_Z):
            z_copy(k, d).wait()
        value = r_z[k, 0].astype(F32)
        for i in range(1, N_Z):
            value = value + r_z[k, i].astype(F32)
        value = value.astype(BF16)
        full[k, my_slab, second, my_rows, :] = value[0:16]
        full[k, my_slab, second, 128:144, :] = value[16:32]
        for d in range(1, N_Z):
            back_z_copy(k, d).start()

    def back_plane(k):
        for d in range(1, N_Z):
            back_z_copy(k, d).wait()
        for dx in range(4):

            @pl.when(reached(k, dx))
            def _(dx=dx):
                for dy in range(N_Y):
                    if dx or dy:
                        plane_copy(k, dx, dy).start()

    def back_core(k):
        @pl.when(sec == k)
        def _():
            back_core_copy(k, 0, 0).start()
            for dx, dy in plane:
                plane_copy(k, dx, dy).wait_recv()
                back_core_copy(k, dx, dy).start()
            pltpu.make_async_copy(
                full.at[k, pl.ds(mine4, 4)], sums_ref.at[pl.ds(mine4, 4)], local.at[D_FULL]
            ).start()

        for dx in range(4):

            @pl.when(reached(k, dx))
            def _(dx=dx):
                for dy in range(N_Y):
                    if dx or dy:
                        plane_copy(k, dx, dy).wait_send()

    def back_end(k):
        @pl.when(sec == k)
        def _():
            for dx in range(4):
                for dy in range(N_Y):
                    back_core_copy(k, dx, dy).wait()
            rest = pltpu.make_async_copy(full.at[k, other], sums_ref.at[other], local.at[D_FULL + 1])
            rest.start()
            pltpu.make_async_copy(
                full.at[k, pl.ds(mine4, 4)], sums_ref.at[pl.ds(mine4, 4)], local.at[D_FULL]
            ).wait()
            rest.wait()

    def own_out(k):
        return pltpu.make_async_copy(o_send.at[k, lat], out_ref.at[k, pl.ds(COLS * lat, COLS)], local.at[D_OUT + k])

    def out_copy(k, d, peer, sample, number):
        return remote(
            o_send.at[k, (lat + d) % 4], out_ref.at[sample, pl.ds(COLS * lat, COLS)], number + d, peer
        )

    def out_start(k, field):
        g3[...] = field[...].reshape(COLS, ROWS, C)
        for a in range(N_LAT):
            o_send[k, a] = g3[:, 4 * a : 4 * a + 4, :].astype(BF16)

        @pl.when(sec == k)
        def _():
            own_out(k).start()
            for d in range(1, 4):
                out_copy(k, d, lat_peer(d), k, S_OWN).start()

        @pl.when(sec != k)
        def _():
            for d in range(4):
                out_copy(k, d, cross_peer(d), 1 - k, S_CROSS).start()

    def out_end(k):
        @pl.when(sec == k)
        def _():
            own_out(k).wait()
            for d in range(1, 4):
                out_copy(k, d, lat_peer(d), k, S_OWN).wait()
            for d in range(4):
                out_copy(k, d, cross_peer(d), 1 - k, S_CROSS).wait_recv()

        @pl.when(sec != k)
        def _():
            for d in range(4):
                out_copy(k, d, cross_peer(d), 1 - k, S_CROSS).wait_send()

    a_x[lat] = x_own[pl.ds(COLS * lat, COLS)]
    for copy in x_in:
        copy.wait()
    gather(a_x, dense)
    copies = halo_start(dense, 0)
    for copy in m_in:
        copy.wait()
    gather_mask()
    sm_in.wait()
    for k in range(2):
        w32[k] = w_sm[k].astype(F32)
    inner_columns(dense, 0, 0, False, u_buf)
    outer_columns(copies, 0, 0, 0, False, u_buf)
    normalise(0)
    up_in.wait()
    their_up = w_up.at[1 - sec, :, up_cols]
    up_fwd = push(their_up, their_up, S_UPF, sibling)
    own_up.wait()
    mlp_hidden(0, 0, 2)
    up_fwd.wait()
    mlp_hidden(0, 2, 4)
    down_in.wait()
    their_down = w_down.at[1 - sec, down_rows]
    down_fwd = push(their_down, their_down, S_DOWNF, sibling)
    own_down.wait()
    mlp_out(0, cot, down_fwd)
    dense[...] = cot[...]
    copies = halo_start(dense, 1)
    c_in = [push(strip(c_ref, (lat + d) % 4), a_c.at[lat], S_C + d - 1, lat_peer(d)) for d in range(1, 4)]
    own_c.start()
    inner_columns(dense, 1, 1, False, u_buf)
    outer_columns(copies, 1, 1, 1, False, u_buf)
    normalise(1)
    mlp_hidden(1, 0, 4)
    mlp_out(1, cot, None)
    out_start(1, cot)

    own_c.wait()
    for copy in c_in:
        copy.wait()
    gather(a_c, cot)
    mlp_back(1)
    copies = halo_start(du_buf, 2)
    first_big(1)
    tap_grads(1)
    core_small(1)
    inner_columns(du_buf, 2, 1, True, u_buf)
    outer_columns(copies, 2, 2, 1, True, u_buf)
    cot[...] = (e_buf[...] + u_buf[...]).astype(BF16).astype(F32)
    first_small(1)

    mlp_back(0)
    copies = halo_start(du_buf, 3)
    first_big(0)
    tap_grads(0)
    core_small(0)
    second_phase(1)
    first_small(0)
    z_phase(1)
    inner_columns(du_buf, 2, 0, True, u_buf)
    second_phase(0)
    outer_columns(copies, 3, 2, 0, True, u_buf)
    z_phase(0)
    cot[...] = (e_buf[...] + u_buf[...]).astype(BF16).astype(F32)
    out_start(0, cot)
    back_z(1)
    back_z(0)
    back_plane(1)
    back_plane(0)
    back_core(1)
    back_core(0)
    out_end(1)
    out_end(0)
    back_end(1)
    back_end(0)


def unpack_kernel(
    sums, raw, out_ref, gup_ref, gdown_ref, taps_ref, chans_ref, bias_ref, held, raw_held, wide, tall, done
):
    loads = [pltpu.make_async_copy(sums.at[i], held.at[i], done.at[i]) for i in range(8)]
    raw_in = pltpu.make_async_copy(raw, raw_held, done.at[24])
    raw_out = pltpu.make_async_copy(raw_held, out_ref, done.at[25])
    for load in loads[:2]:
        load.start()
    raw_in.start()
    for load in loads[2:]:
        load.start()
    stores = []
    for i in range(8):
        loads[i].wait()
        cols = pl.ds(128 * i, 128)
        for g in range(2):
            part = slice(128 * g, 128 * (g + 1))
            wide[i, part, :] = held[i, g, 0:128, :].astype(F32) * factor
            tall[i, :, part] = held[i, 2 + g, 0:128, :].astype(F32) * factor
        stores.append(pltpu.make_async_copy(wide.at[i], gup_ref.at[:, cols], done.at[8 + i]))
        stores.append(pltpu.make_async_copy(tall.at[i], gdown_ref.at[cols], done.at[16 + i]))
        stores[-2].start()
        stores[-1].start()
        if i == 2:
            raw_in.wait()
            raw_out.start()
        piece = held[i, 0, 128:144, :].astype(F32) * factor
        bias_ref[:, 128 * i : 128 * (i + 1)] = piece[14:15]
        for h in range(2):
            lanes = slice(128 * h, 128 * (h + 1))
            if i < 7:
                for q in range(7):
                    taps_ref[7 * i + q, :, lanes] = piece[7 * h + q : 7 * h + q + 1]
            else:
                for r in range(5):
                    chans_ref[r, :, lanes] = piece[5 * h + r : 5 * h + r + 1]
    raw_out.wait()
    for store in stores:
        store.wait()


def on_device(
    window_input,
    output_cotangent,
    ocean_mask,
    dw_kernel,
    channel_params,
    up_weight,
    up_bias,
    down_weight,
):
    vmem = pl.BlockSpec(memory_space=pltpu.VMEM)
    hbm = pl.BlockSpec(memory_space=pl.ANY)
    raw, sums = pl.pallas_call(
        step_kernel,
        out_shape=(
            jax.ShapeDtypeStruct((2, PART, 4, C), BF16),
            jax.ShapeDtypeStruct((8, 4, 144, 128), BF16),
        ),
        in_specs=[hbm, hbm, vmem, vmem, vmem, vmem, hbm, hbm],
        out_specs=(hbm, hbm),
        scratch_shapes=[
            pltpu.VMEM((2, 256, 1024), BF16),
            pltpu.VMEM((2, 1024, 256), BF16),
            pltpu.VMEM((2, 80, C), BF16),
            pltpu.VMEM((2, 80, C), F32),
            pltpu.VMEM((80, C), F32),
            pltpu.VMEM((8, 128), F32),
            pltpu.VMEM((PART, 4, C), BF16),
            pltpu.VMEM((4, COLS, 4, C), BF16),
            pltpu.VMEM((4, COLS, 4, C), BF16),
            pltpu.VMEM((4, 8, 128), F32),
            pltpu.VMEM((COLS, ROWS, C), F32),
            pltpu.VMEM((CELLS, C), F32),
            pltpu.VMEM((CELLS, 128), F32),
            pltpu.VMEM((COLS + 6, 32, C), F32),
            pltpu.VMEM((3, 7, COLS + 6, ROWS, C), F32),
            pltpu.VMEM((4, 2, EDGE, C), BF16),
            pltpu.VMEM((4, 2, EDGE, C), BF16),
            pltpu.VMEM((CELLS, C), F32),
            pltpu.VMEM((2, CELLS, C), F32),
            pltpu.VMEM((2, CELLS, 1), F32),
            pltpu.VMEM((2, CELLS, C), BF16),
            pltpu.VMEM((2, CELLS, 1024), BF16),
            pltpu.VMEM((2, CELLS, 1024), F32),
            pltpu.VMEM((2, CELLS, C), F32),
            pltpu.VMEM((CELLS, C), F32),
            pltpu.VMEM((CELLS, C), BF16),
            pltpu.VMEM((CELLS, C), F32),
            pltpu.VMEM((CELLS, C), F32),
            pltpu.VMEM((2, 8, SLAB, 128), BF16),
            pltpu.VMEM((8, 16, 128), F32),
            pltpu.VMEM((2, 4, SLAB, 128), BF16),
            pltpu.VMEM((2, 4, SLAB, 128), BF16),
            pltpu.VMEM((2, 3, SLAB, 128), BF16),
            pltpu.VMEM((2, 4, 144, 128), BF16),
            pltpu.VMEM((2, 4, 144, 128), BF16),
            pltpu.VMEM((2, 8, 32, 128), BF16),
            pltpu.VMEM((2, 8, 32, 128), BF16),
            pltpu.VMEM((2, 8, 4, 144, 128), BF16),
            pltpu.VMEM((2, 4, COLS, 4, C), BF16),
            pltpu.SemaphoreType.DMA((N_LOCAL,)),
            pltpu.SemaphoreType.DMA((N_SEM,)),
            pltpu.SemaphoreType.DMA((N_SEM,)),
        ],
        compiler_params=pltpu.CompilerParams(
            collective_id=0, has_side_effects=True, vmem_limit_bytes=56 << 20
        ),
        name="two_blocks",
    )(
        window_input.transpose(0, 2, 1, 3),
        output_cotangent.transpose(0, 2, 1, 3),
        ocean_mask,
        dw_kernel[0],
        channel_params[0],
        up_bias,
        up_weight[0],
        down_weight[0],
    )
    boundary, gup, gdown, taps, chans, gbias = pl.pallas_call(
        unpack_kernel,
        out_shape=(
            jax.ShapeDtypeStruct((2, PART, 4, C), BF16),
            jax.ShapeDtypeStruct((256, 1024), F32),
            jax.ShapeDtypeStruct((1024, 256), F32),
            jax.ShapeDtypeStruct((49, 1, C), F32),
            jax.ShapeDtypeStruct((5, 1, C), F32),
            jax.ShapeDtypeStruct((1, 1024), F32),
        ),
        in_specs=[hbm, hbm],
        out_specs=(hbm, hbm, hbm, vmem, vmem, vmem),
        scratch_shapes=[
            pltpu.VMEM((8, 4, 144, 128), BF16),
            pltpu.VMEM((2, PART, 4, C), BF16),
            pltpu.VMEM((8, 256, 128), F32),
            pltpu.VMEM((8, 128, 256), F32),
            pltpu.SemaphoreType.DMA((26,)),
        ],
        compiler_params=pltpu.CompilerParams(vmem_limit_bytes=60 << 20),
        name="unpack",
    )(sums, raw)
    return (
        boundary.transpose(0, 2, 1, 3)[None],
        taps.transpose(1, 0, 2),
        chans.transpose(1, 0, 2),
        gup[None],
        gbias,
        gdown[None],
    )


def solution(mesh):
    in_specs = (
        P(None, "lat", "lon", None),
        P(None, "lat", "lon", None),
        P("lat", "lon"),
        P("section", None, None),
        P("section", None, None),
        P("section", None, None),
        P("section", None),
        P("section", None, None),
    )
    out_specs = (
        P("section", None, "lat", "lon", None),
        P("section", None, None),
        P("section", None, None),
        P("section", None, None),
        P("section", None),
        P("section", None, None),
    )
    return jax.shard_map(
        on_device, mesh=mesh, in_specs=in_specs, out_specs=out_specs, check_vma=False
    )
```
